128 devices in a mesh: ctx: 8 (over x_lo, y), exp: 16 (over z, x_hi, core).
Axes of the slice: x: 4 (x_hi: 2, x_lo: 2; x = x_hi * 2 + x_lo), y: 4, z: 4, core: 2. Of those that a mesh axis runs over, the one named last changes fastest.
Arguments:
- queries: bfloat16 [16, 1024, 4096], P('exp', 'ctx'), may hold values from -6 to 6
- keys: bfloat16 [16, 1024, 512], P('exp', 'ctx'), may hold values from -6 to 6
- values: bfloat16 [16, 1024, 512], P('exp', 'ctx'), may hold values from -8 to 8
- resid: bfloat16 [16, 1024, 2048], P('exp', 'ctx'), may hold values from -40 to 40
- out_weight: bfloat16 [4096, 2048], P('ctx', 'exp'), may hold values from -0.5 to 0.5
- norm_gain: float32 [2048], replicated, may hold values from 0.5 to 2
- expert_gate: bfloat16 [32, 2048, 768], P('exp'), may hold values from -0.125 to 0.125
- expert_up: bfloat16 [32, 2048, 768], P('exp'), may hold values from -0.125 to 0.125
- expert_down: bfloat16 [32, 768, 2048], P('exp'), may hold values from -0.4375 to 0.4375
- route_ids: int32 [16, 1024, 8], P('exp', 'ctx'), may hold values from 0 to 31, as said below
- route_gates: float32 [16, 1024, 8], P('exp', 'ctx'), may hold values from 0.1 to 1
Outputs:
- attn_resid: bfloat16 [16, 1024, 2048], P('exp', 'ctx')
- layer_out: bfloat16 [16, 1024, 2048], P('exp', 'ctx')
The draws below stay inside these ranges and needn't reach their ends.
Inputs may be any that keep to these rules, and one draw needn't show every extreme that they name: `route_ids`: each row names 8 different experts. In every block of 128 consecutive positions of a sequence (the tokens of one device) each expert is named by at most 64 rows, and one expert, the same in all blocks of a draw, by exactly 64 rows.
All inputs are finite; a program needn't handle non-finite values.
Results may differ from the reference program's by a relative error of at most 0.017.
Values may be sent and summed in bfloat16 or wider, within the bound.
A program may use at most 128 MiB of HBM per device.

```python
import math
import jax
import jax.numpy as jnp
from jax import lax

D = 2048
QUERY_HEAD_COUNT = 32
KEY_VALUE_HEADS = 4
HEAD_SIZE = 128
FF = 768
TOPK = 8
TOK_DEV = 128
SEQUENCE_LENGTH = 1024
SEQUENCE_COUNT = 16
EXPERTS = 32
CAP = 64


def draw_queries(key, part):
    start_offset = jnp.clip(jax.random.normal(jax.random.fold_in(key, 11), (SEQUENCE_COUNT, SEQUENCE_LENGTH, QUERY_HEAD_COUNT * HEAD_SIZE), jnp.float32), -4.0, 4.0)
    return start_offset.astype(jnp.bfloat16)


def draw_keys(key, part):
    start_offset = jnp.clip(jax.random.normal(jax.random.fold_in(key, 12), (SEQUENCE_COUNT, SEQUENCE_LENGTH, KEY_VALUE_HEADS * HEAD_SIZE), jnp.float32), -4.0, 4.0)
    return start_offset.astype(jnp.bfloat16)


def draw_resid(key, part):
    start_offset = jnp.clip(jax.random.normal(jax.random.fold_in(key, 41), (SEQUENCE_COUNT, SEQUENCE_LENGTH, D), jnp.float32), -4.0, 4.0)
    low = jnp.log(0.3)
    high = jnp.log(3.0)
    row_scale = jnp.exp(jax.random.uniform(jax.random.fold_in(key, 42), (SEQUENCE_COUNT, SEQUENCE_LENGTH, 1), jnp.float32, low, high))
    column_scale = jnp.exp(jax.random.uniform(jax.random.fold_in(key, 43), (1, 1, D), jnp.float32, low, high))
    return jnp.clip(start_offset * row_scale * column_scale, -40.0, 40.0).astype(jnp.bfloat16)


def draw_route_ids(key, part):
    block_total = SEQUENCE_COUNT * (SEQUENCE_LENGTH // TOK_DEV)
    hot_expert = jax.random.randint(jax.random.fold_in(key, 31), (), 0, EXPERTS)
    block_keys = jax.random.split(jax.random.fold_in(key, 32), block_total)

    def one_block(block_key):
        cycle = jax.random.permutation(jax.random.fold_in(block_key, 1), EXPERTS - 1).astype(jnp.int32)
        token_order = jax.random.permutation(jax.random.fold_in(block_key, 2), TOK_DEV).astype(jnp.int32)
        turn = jax.random.randint(jax.random.fold_in(block_key, 3), (TOK_DEV, 1), 0, TOPK)
        place = jnp.arange(TOK_DEV, dtype=jnp.int32)[:, None]
        column = jnp.arange(TOPK, dtype=jnp.int32)[None, :]
        is_hot = place < CAP
        index_hot = place * (TOPK - 1) + column - 1
        index_rest = CAP * (TOPK - 1) + (place - CAP) * TOPK + column
        entry = jnp.where(is_hot, index_hot, index_rest)
        others = cycle[jnp.mod(entry, EXPERTS - 1)]
        others = others + (others >= hot_expert).astype(jnp.int32)
        picked = jnp.where(is_hot & (column == 0), hot_expert, others)
        rotated = jnp.take_along_axis(picked, jnp.mod(column + turn, TOPK), axis=1)
        return jnp.zeros((TOK_DEV, TOPK), jnp.int32).at[token_order].set(rotated)
    return jax.vmap(one_block)(block_keys).reshape(SEQUENCE_COUNT, SEQUENCE_LENGTH, TOPK)


def block_scale(stream_key, extent, pieces, low, high):
    def one(dim, blocks):
        heights = jax.random.uniform(jax.random.fold_in(jax.random.fold_in(stream_key, 6), dim), (blocks,), jnp.float32, low / len(pieces), high / len(pieces))
        return jnp.repeat(jnp.exp(heights), extent[dim] // blocks).reshape((-1,) + (1,) * (len(extent) - dim - 1))

    factor_of = one(*pieces[0])
    for cut in pieces[1:]:
        factor_of = factor_of * one(*cut)
    return factor_of


def gaussian(own_key, dims, deviation, limit, cuts=(), held_as=jnp.bfloat16):
    loudness = block_scale(own_key, dims, cuts, -0.22, 0.18) if cuts else 1.0
    values = jax.random.normal(own_key, dims, jnp.float32) * deviation * loudness
    return jnp.minimum(jnp.maximum(values, -limit), limit).astype(held_as)


def setup_inputs(seed: int = 0) -> dict:
    key_of = jax.random.split(jax.random.key(seed), 12)
    queries = draw_queries(jax.random.fold_in(key_of[11], 71), 0)
    keys = draw_keys(jax.random.fold_in(key_of[11], 71), 0)
    values = gaussian(key_of[2], (SEQUENCE_COUNT, SEQUENCE_LENGTH, KEY_VALUE_HEADS * HEAD_SIZE), 2.0, 8.0, ((0, 16), (1, 8)))
    resid = draw_resid(jax.random.fold_in(key_of[11], 71), 0)
    out_weight = gaussian(key_of[4], (QUERY_HEAD_COUNT * HEAD_SIZE, D), HEAD_SIZE ** -0.5, 0.5, ((0, 8), (1, 16)))
    norm_gain = jnp.clip(jnp.exp(jax.random.uniform(key_of[5], (D,), jnp.float32, math.log(0.5), math.log(2.0))), 0.5, 2.0)
    expert_gate = gaussian(key_of[6], (EXPERTS, D, FF), D ** -0.5, 0.125, ((0, 16),))
    expert_up = gaussian(key_of[7], (EXPERTS, D, FF), D ** -0.5, 0.125, ((0, 16),))
    expert_down = gaussian(key_of[8], (EXPERTS, FF, D), (FF // 4) ** -0.5, 0.4375, ((0, 16),))
    route_ids = draw_route_ids(jax.random.fold_in(key_of[11], 71), 0)
    route_gates = jnp.clip(0.1 + 0.9 * jax.random.uniform(key_of[10], (SEQUENCE_COUNT, SEQUENCE_LENGTH, TOPK), jnp.float32) ** block_scale(key_of[10], (SEQUENCE_COUNT, SEQUENCE_LENGTH, TOPK), ((0, 16), (1, 8)), -0.2, 0.2), 0.1, 1.0)
    return {"queries": queries, "keys": keys, "values": values, "resid": resid, "out_weight": out_weight, "norm_gain": norm_gain, "expert_gate": expert_gate, "expert_up": expert_up, "expert_down": expert_down, "route_ids": route_ids, "route_gates": route_gates}


norm_eps = 1e-06
tile_height = 256

def attend_sequence(inputs):
    query_sequence, key_sequence, value_sequence = inputs
    sequence_length = query_sequence.shape[0]
    query_group = QUERY_HEAD_COUNT // KEY_VALUE_HEADS
    query_head_rows = query_sequence.reshape(sequence_length, KEY_VALUE_HEADS, query_group, HEAD_SIZE).astype(jnp.float32)
    key_head_rows = key_sequence.reshape(sequence_length, KEY_VALUE_HEADS, HEAD_SIZE).astype(jnp.float32)
    value_head_rows = value_sequence.reshape(sequence_length, KEY_VALUE_HEADS, HEAD_SIZE).astype(jnp.float32)
    raw_scores = jnp.einsum('tngd,und->ngtu', query_head_rows, key_head_rows) * HEAD_SIZE ** (-0.5)
    position = jnp.arange(sequence_length, dtype=jnp.int32)
    allowed = position[:, None] >= position[None, :]
    masked = jnp.where(allowed, raw_scores, -jnp.inf)
    row_top = lax.optimization_barrier(jnp.max(masked, axis=-1, keepdims=True))
    exp_scores = jnp.where(allowed, jnp.exp(masked - row_top), 0.0)
    row_total = lax.optimization_barrier(jnp.sum(exp_scores, axis=-1))
    weights = exp_scores.astype(jnp.bfloat16).astype(jnp.float32)
    attended = jnp.einsum('ngtu,und->ngtd', weights, value_head_rows) / row_total[..., None]
    return attended.transpose(2, 0, 1, 3).reshape(sequence_length, QUERY_HEAD_COUNT * HEAD_SIZE).astype(jnp.bfloat16)

def reference(queries, keys, values, resid, out_weight, norm_gain, expert_gate, expert_up, expert_down, route_ids, route_gates):
    attention = lax.map(attend_sequence, (queries, keys, values))
    token_count = SEQUENCE_COUNT * SEQUENCE_LENGTH
    projected = jnp.dot(attention.reshape(token_count, QUERY_HEAD_COUNT * HEAD_SIZE), out_weight, preferred_element_type=jnp.float32)
    attn_resid = (resid.reshape(token_count, D).astype(jnp.float32) + projected).astype(jnp.bfloat16)
    resid_wide = attn_resid.astype(jnp.float32)
    scale_row = lax.rsqrt(lax.optimization_barrier(jnp.mean(resid_wide * resid_wide, axis=-1, keepdims=True)) + norm_eps)
    normed = (resid_wide * scale_row * norm_gain).astype(jnp.bfloat16)
    route_list = route_ids.reshape(token_count, TOPK)
    gate_rows = route_gates.reshape(token_count, TOPK)
    shares = gate_rows / lax.optimization_barrier(jnp.sum(gate_rows, axis=-1, keepdims=True))
    entry_count = token_count * TOPK
    entry_expert = route_list.reshape(entry_count)
    sort_order = jnp.argsort(entry_expert, stable=True).astype(jnp.int32)
    expert_range = jnp.arange(EXPERTS, dtype=jnp.int32)
    counts = lax.optimization_barrier(jnp.sum((entry_expert[:, None] == expert_range[None, :]).astype(jnp.int32), axis=0))
    group_first = jnp.cumsum(counts) - counts
    group_blocks = (counts + tile_height - 1) // tile_height
    block_first = jnp.cumsum(group_blocks) - group_blocks
    sorted_expert = entry_expert[sort_order]
    group_rank = jnp.arange(entry_count, dtype=jnp.int32) - group_first[sorted_expert]
    padded_place = block_first[sorted_expert] * tile_height + group_rank
    block_count = (entry_count + tile_height - 1) // tile_height + EXPERTS
    row_token = jnp.full((block_count * tile_height,), token_count, jnp.int32)
    row_token = row_token.at[padded_place].set(sort_order // TOPK)
    block_index = jnp.arange(block_count, dtype=jnp.int32)
    block_expert = lax.optimization_barrier(jnp.sum((block_first[None, :] <= block_index[:, None]).astype(jnp.int32), axis=1)) - 1
    normed_padded = jnp.concatenate([normed, jnp.zeros((1, D), jnp.bfloat16)], axis=0)

    def run_block(inputs):
        tokens_here, expert_here = inputs
        arrived = normed_padded[tokens_here].astype(jnp.float32)
        gate_part = jnp.dot(arrived, expert_gate[expert_here].astype(jnp.float32))
        up_part = jnp.dot(arrived, expert_up[expert_here].astype(jnp.float32))
        activated = (jax.nn.silu(gate_part) * up_part).astype(jnp.bfloat16)
        return jnp.dot(activated.astype(jnp.float32), expert_down[expert_here].astype(jnp.float32)).astype(jnp.bfloat16)
    block_out = lax.map(run_block, (row_token.reshape(block_count, tile_height), block_expert))
    flat_out = block_out.reshape(block_count * tile_height, D)
    entry_place = jnp.zeros((entry_count,), jnp.int32).at[sort_order].set(padded_place).reshape(token_count, TOPK)
    combined = resid_wide
    for column in range(TOPK):
        combined = combined + shares[:, column:column + 1] * flat_out[entry_place[:, column]].astype(jnp.float32)
    layer_out = combined.astype(jnp.bfloat16)
    return (attn_resid.reshape(SEQUENCE_COUNT, SEQUENCE_LENGTH, D), layer_out.reshape(SEQUENCE_COUNT, SEQUENCE_LENGTH, D))
```

```python
import functools

import jax
import jax.numpy as jnp
from jax import lax
from jax.experimental import pallas as pl
from jax.experimental.pallas import tpu as pltpu
from jax.sharding import PartitionSpec as P

QUERY_HEAD_COUNT = 32
KEY_VALUE_HEADS = 4
HEAD_SIZE = 128
TOPK = 8
CAP = 64
TOK = 128
D = 2048
FF = 768
EXPERTS = 32
MESH = pl.DeviceIdType.MESH

norm_eps = 1e-06
mask_fill_value = -1e30

RELATIONS = ((0, 0), (3, 0), (1, 0), (0, 1), (2, 0), (3, 1), (1, 1), (2, 1))
PAIRS = ((0, 3), (1, 2), (4, 7), (5, 6))


def moe_kernel(
    normed_ref,
    resid_ref,
    share_ref,
    gate_hbm,
    up_hbm,
    down_hbm,
    out_ref,
    gate_w,
    up_w,
    down_w,
    blocks,
    parts,
    sib_parts,
    half_in,
    full_in,
    far_in,
    hop_in,
    slots_in,
    slots_out,
    act,
    weight_sem,
    ag_send,
    ag_recv,
    sib_send,
    sib_recv,
    part_send,
    part_recv,
    rs_send,
    rs_recv,
):
    me = lax.axis_index("exp")
    z, xh, core = me // 4, lax.rem(me // 2, 2), lax.rem(me, 2)

    def block_of(relation, which):
        dz, dx = RELATIONS[relation]
        return lax.rem(z + dz, 4) * 4 + lax.rem(xh + dx, 2) * 2 + which

    other = 1 - core
    sibling = me + 1 - 2 * core
    z_up, z_down, x_over = block_of(2, core), block_of(1, core), block_of(3, core)

    loads = []
    for number, (src, dst) in enumerate(((gate_hbm, gate_w), (up_hbm, up_w), (down_hbm, down_w))):
        loads.append(pltpu.make_async_copy(src, dst, weight_sem.at[number]))
        loads[-1].start()
    blocks[me] = normed_ref[...]

    barrier = pltpu.get_barrier_semaphore()
    for peer in (sibling, z_up, z_down, x_over):
        pl.semaphore_signal(barrier, inc=1, device_id={"exp": peer}, device_id_type=MESH)
    pl.semaphore_wait(barrier, 4)

    def send(src, dst, sems, number, peer):
        return pltpu.make_async_remote_copy(
            src_ref=src,
            dst_ref=dst,
            send_sem=sems[0].at[number],
            recv_sem=sems[1].at[number],
            device_id={"exp": peer},
            device_id_type=MESH,
        )

    ag = (ag_send, ag_recv)
    sib = (sib_send, sib_recv)
    part = (part_send, part_recv)
    rs = (rs_send, rs_recv)
    low, high = pl.ds(0, CAP), pl.ds(CAP, CAP)

    def whole(relation):
        return blocks.at[block_of(relation, core)]

    def half(relation, rows):
        return blocks.at[block_of(relation, core), rows]

    ag_out = (
        send(whole(0), whole(0), ag, 0, z_up),
        send(whole(0), whole(0), ag, 1, z_down),
        send(whole(0), whole(0), ag, 2, x_over),
        send(half(1, low), half(1, low), ag, 3, z_up),
        send(half(2, high), half(2, high), ag, 4, z_down),
        send(whole(3), whole(3), ag, 5, z_up),
        send(whole(3), whole(3), ag, 6, z_down),
        send(whole(4), whole(4), ag, 7, x_over),
    )
    ag_in = (
        send(whole(1), whole(1), ag, 0, z_up),
        send(whole(2), whole(2), ag, 1, z_down),
        send(whole(3), whole(3), ag, 2, x_over),
        send(half(4, low), half(4, low), ag, 3, z_up),
        send(half(4, high), half(4, high), ag, 4, z_down),
        send(whole(5), whole(5), ag, 5, z_up),
        send(whole(6), whole(6), ag, 6, z_down),
        send(whole(7), whole(7), ag, 7, x_over),
    )
    sib_out = [send(whole(k), whole(k), sib, k, sibling) for k in range(8)]
    sib_in = []
    for k in range(8):
        arriving = blocks.at[block_of(k, other)]
        sib_in.append(send(arriving, arriving, sib, k, sibling))

    for number in (0, 1, 2):
        ag_out[number].start()
    sib_out[0].start()
    for load in loads:
        load.wait()

    lane = lax.broadcasted_iota(jnp.int32, (TOK, TOK), 1)
    row = lax.broadcasted_iota(jnp.int32, (TOK, TOK), 0)
    up_to = (row <= lane).astype(jnp.bfloat16)
    slot_of_row = lax.rem(row, CAP).astype(jnp.float32)

    def part_copy(chip):
        return send(parts.at[chip * 2 + other], sib_parts.at[chip], part, chip, sibling)

    def selection(block):
        both = share_ref[block]
        chosen = both > 0.0
        count = jnp.dot(
            chosen.astype(jnp.bfloat16), up_to, preferred_element_type=jnp.float32
        )
        place = jnp.where(chosen, count - 1.0, -1.0)
        place_rows = jnp.concatenate(
            [jnp.broadcast_to(place[j : j + 1], (CAP, TOK)) for j in range(2)], axis=0
        )
        share_rows = jnp.concatenate(
            [jnp.broadcast_to(both[j : j + 1], (CAP, TOK)) for j in range(2)], axis=0
        )
        picked = place_rows == slot_of_row
        slot_share = jnp.sum(jnp.where(picked, share_rows, 0.0), axis=1, keepdims=True)
        return picked.astype(jnp.float32), slot_share

    def step(number, carry):
        @pl.when(number == 0)
        def _():
            ag_in[0].wait_recv()
            ag_out[3].start()
            sib_out[1].start()
            ag_in[1].wait_recv()
            ag_out[4].start()
            sib_out[2].start()
            ag_in[2].wait_recv()
            ag_out[5].start()
            ag_out[6].start()
            sib_out[3].start()
            sib_in[0].wait_recv()
            sib_in[3].wait_recv()

        @pl.when(number == 1)
        def _():
            ag_in[3].wait_recv()
            ag_in[4].wait_recv()
            ag_out[7].start()
            sib_out[4].start()
            sib_in[1].wait_recv()
            sib_in[2].wait_recv()

        @pl.when(number == 2)
        def _():
            ag_in[5].wait_recv()
            sib_out[5].start()
            ag_in[6].wait_recv()
            sib_out[6].start()
            ag_in[7].wait_recv()
            sib_out[7].start()
            sib_in[4].wait_recv()
            sib_in[7].wait_recv()

        @pl.when(number == 3)
        def _():
            sib_in[5].wait_recv()
            sib_in[6].wait_recv()

        def chip_at(which):
            dz, dx = 0, 0
            for k, pair in enumerate(PAIRS):
                here = RELATIONS[pair[which]]
                dz = jnp.where(number == k, here[0], dz)
                dx = jnp.where(number == k, here[1], dx)
            return lax.rem(z + dz, 4) * 2 + lax.rem(xh + dx, 2)

        chips = (chip_at(0), chip_at(1))
        sources = [chips[q // 2] * 2 + q % 2 for q in range(4)]
        for q in range(4):
            picked, _ = selection(sources[q])
            found = jnp.dot(
                picked.astype(jnp.bfloat16),
                blocks[sources[q]],
                preferred_element_type=jnp.float32,
            ).astype(jnp.bfloat16)
            for j in range(2):
                slots_in[j, q * CAP : (q + 1) * CAP] = found[j * CAP : (j + 1) * CAP]

        def expert(j, carry):
            for n in range(3):
                cols = slice(n * 256, (n + 1) * 256)
                gate_part = jnp.dot(
                    slots_in[j], gate_w[j, :, cols], preferred_element_type=jnp.float32
                )
                up_part = jnp.dot(
                    slots_in[j], up_w[j, :, cols], preferred_element_type=jnp.float32
                )
                act[:, cols] = (gate_part / (1.0 + jnp.exp(-gate_part)) * up_part).astype(
                    jnp.bfloat16
                )
            for n in range(4):
                cols = slice(n * 512, (n + 1) * 512)
                result = jnp.dot(act[...], down_w[j, :, cols], preferred_element_type=jnp.float32)
                for q in range(4):
                    slots_out[q, pl.ds(pl.multiple_of(j * CAP, CAP), CAP), cols] = result[
                        q * CAP : (q + 1) * CAP
                    ].astype(jnp.bfloat16)
            return carry

        lax.fori_loop(0, 2, expert, 0)
        for q in range(4):
            picked, slot_share = selection(sources[q])
            scaled = (slots_out[q].astype(jnp.float32) * slot_share).astype(jnp.bfloat16)
            parts[sources[q]] = jnp.dot(
                picked.T.astype(jnp.bfloat16), scaled, preferred_element_type=jnp.float32
            ).astype(jnp.bfloat16)
            if q % 2:
                part_copy(chips[q // 2]).start()
        return carry

    lax.fori_loop(0, 4, step, 0)

    def chip_sum(relation):
        dz, dx = RELATIONS[relation]
        chip = lax.rem(z + dz, 4) * 2 + lax.rem(xh + dx, 2)
        pltpu.make_async_remote_copy(
            src_ref=parts.at[chip * 2 + other],
            dst_ref=sib_parts.at[chip],
            send_sem=part_send.at[chip],
            recv_sem=part_recv.at[chip],
            device_id={"exp": sibling},
            device_id_type=MESH,
        ).wait_recv()
        add_into(chip * 2 + core, slice(None), sib_parts.at[chip])

    def add_into(block, rows, extra):
        parts[block, rows] = (
            parts[block, rows].astype(jnp.float32) + extra[...].astype(jnp.float32)
        ).astype(jnp.bfloat16)

    def part_of(relation):
        return parts.at[block_of(relation, core)]

    chip_sum(7)
    rs_out = [send(part_of(7), hop_in, rs, 0, x_over)]
    rs_out[0].start()
    chip_sum(5)
    rs_out.append(send(part_of(5), full_in.at[2], rs, 1, z_down))
    rs_out[1].start()
    chip_sum(6)
    rs_out.append(send(part_of(6), full_in.at[3], rs, 2, z_up))
    rs_out[2].start()
    chip_sum(4)
    rs_out[0].wait_recv()
    add_into(block_of(4, core), slice(None), hop_in)
    rs_out.append(
        send(parts.at[block_of(4, core), low], half_in.at[0], rs, 3, z_down)
    )
    rs_out[3].start()
    rs_out.append(send(parts.at[block_of(4, core), high], half_in.at[1], rs, 4, z_up))
    rs_out[4].start()
    chip_sum(3)
    chip_sum(1)
    chip_sum(2)
    chip_sum(0)
    rs_out[1].wait_recv()
    add_into(block_of(3, core), slice(None), full_in.at[2])
    rs_out[2].wait_recv()
    add_into(block_of(3, core), slice(None), full_in.at[3])
    rs_out.append(send(part_of(3), far_in, rs, 5, x_over))
    rs_out[5].start()
    rs_out[3].wait_recv()
    add_into(block_of(1, core), slice(0, CAP), half_in.at[0])
    rs_out.append(send(part_of(1), full_in.at[0], rs, 6, z_down))
    rs_out[6].start()
    rs_out[4].wait_recv()
    add_into(block_of(2, core), slice(CAP, TOK), half_in.at[1])
    rs_out.append(send(part_of(2), full_in.at[1], rs, 7, z_up))
    rs_out[7].start()

    rs_out[6].wait_recv()
    rs_out[7].wait_recv()
    rs_out[5].wait_recv()
    total = resid_ref[...].astype(jnp.float32) + parts[me].astype(jnp.float32)
    for extra in (full_in.at[0], full_in.at[1], far_in):
        total = total + extra[...].astype(jnp.float32)
    out_ref[...] = total.astype(jnp.bfloat16)

    for copy in (*ag_out, *sib_out, *rs_out):
        copy.wait_send()
    for chip in range(8):
        part_copy(chip).wait_send()


def moe(normed, attn_resid, shares, expert_gate, expert_up, expert_down):
    vmem = pl.BlockSpec(memory_space=pltpu.VMEM)
    hbm = pl.BlockSpec(memory_space=pl.ANY)
    dma = pltpu.SemaphoreType.DMA
    bf16 = jnp.bfloat16
    return pl.pallas_call(
        moe_kernel,
        out_shape=jax.ShapeDtypeStruct((TOK, D), bf16),
        in_specs=[vmem, vmem, vmem, hbm, hbm, hbm],
        out_specs=vmem,
        scratch_shapes=[
            pltpu.VMEM((2, D, FF), bf16),
            pltpu.VMEM((2, D, FF), bf16),
            pltpu.VMEM((2, FF, D), bf16),
            pltpu.VMEM((16, TOK, D), bf16),
            pltpu.VMEM((16, TOK, D), bf16),
            pltpu.VMEM((8, TOK, D), bf16),
            pltpu.VMEM((2, CAP, D), bf16),
            pltpu.VMEM((4, TOK, D), bf16),
            pltpu.VMEM((TOK, D), bf16),
            pltpu.VMEM((TOK, D), bf16),
            pltpu.VMEM((2, 256, D), bf16),
            pltpu.VMEM((4, TOK, D), bf16),
            pltpu.VMEM((256, FF), bf16),
            dma((3,)),
            dma((8,)),
            dma((8,)),
            dma((8,)),
            dma((8,)),
            dma((8,)),
            dma((8,)),
            dma((8,)),
            dma((8,)),
        ],
        compiler_params=pltpu.CompilerParams(
            collective_id=1, has_side_effects=True, vmem_limit_bytes=60 << 20
        ),
    )(normed, attn_resid, shares, expert_gate, expert_up, expert_down)


def from_behind(shard, axis, by):
    devices = lax.axis_size(axis)
    pairs = [(i, i + by) for i in range(devices) if 0 <= i + by < devices]
    return lax.ppermute(shard, axis, pairs)


def attend_block(state_now, key_value_portion, begin_row, query_head_rows, query_place):
    row_top, row_total, accum = state_now
    key_total = key_value_portion.shape[1]
    key_head_rows = key_value_portion[0].reshape(key_total, KEY_VALUE_HEADS, HEAD_SIZE)
    value_head_rows = key_value_portion[1].reshape(key_total, KEY_VALUE_HEADS, HEAD_SIZE)
    raw_scores = jnp.einsum(
        "tngd,und->ngtu", query_head_rows, key_head_rows, preferred_element_type=jnp.float32
    ) * HEAD_SIZE ** (-0.5)
    key_place = begin_row + jnp.arange(key_total, dtype=jnp.int32)
    allowed = query_place[:, None] >= key_place[None, :]
    raw_scores = jnp.where(allowed, raw_scores, mask_fill_value)
    new_top = jnp.maximum(row_top, jnp.max(raw_scores, axis=-1))
    factor = jnp.exp(row_top - new_top)
    exp_scores = jnp.where(allowed, jnp.exp(raw_scores - new_top[..., None]), 0.0)
    row_total = row_total * factor + jnp.sum(exp_scores, axis=-1)
    weights = exp_scores.astype(jnp.bfloat16)
    accum = accum * factor[..., None] + jnp.einsum(
        "ngtu,und->ngtd", weights, value_head_rows, preferred_element_type=jnp.float32
    )
    return (new_top, row_total, accum)


def local(
    queries,
    keys,
    values,
    resid,
    out_weight,
    norm_gain,
    expert_gate,
    expert_up,
    expert_down,
    route_ids,
    route_gates,
):
    token_rows = queries.shape[1]
    ctx_count = lax.axis_size("ctx")
    exp_count = lax.axis_size("exp")
    my_block = lax.axis_index("ctx")
    query_group = QUERY_HEAD_COUNT // KEY_VALUE_HEADS
    query_head_rows = queries[0].reshape(token_rows, KEY_VALUE_HEADS, query_group, HEAD_SIZE)
    query_place = my_block * token_rows + jnp.arange(token_rows, dtype=jnp.int32)
    kv_local = jnp.stack([keys[0], values[0]])
    state_first = (
        jnp.full((KEY_VALUE_HEADS, query_group, token_rows), mask_fill_value, jnp.float32),
        jnp.zeros((KEY_VALUE_HEADS, query_group, token_rows), jnp.float32),
        jnp.zeros((KEY_VALUE_HEADS, query_group, token_rows, HEAD_SIZE), jnp.float32),
    )
    state_now = attend_block(
        state_first, kv_local, my_block * token_rows, query_head_rows, query_place
    )

    def circle_step(step_num, carried):
        state_in, key_value_portion = carried
        key_value_portion = from_behind(key_value_portion, "ctx", 1)
        source = my_block - step_num
        state_out = lax.cond(
            source >= 0,
            lambda held: attend_block(
                held, key_value_portion, source * token_rows, query_head_rows, query_place
            ),
            lambda held: held,
            state_in,
        )
        return (state_out, key_value_portion)

    state_now, kv_last = lax.fori_loop(1, ctx_count, circle_step, (state_now, kv_local))
    row_top, row_total, accum = state_now
    attention = (
        (accum / row_total[..., None])
        .transpose(2, 0, 1, 3)
        .reshape(token_rows, QUERY_HEAD_COUNT * HEAD_SIZE)
        .astype(jnp.bfloat16)
    )
    all_rows = lax.all_gather(out_weight, "ctx", axis=0, tiled=True)
    projected = jnp.dot(
        attention,
        lax.all_gather(all_rows, "exp", axis=1, tiled=True),
        preferred_element_type=jnp.float32,
    )
    attn_resid = (resid[0].astype(jnp.float32) + projected).astype(jnp.bfloat16)
    resid_wide = attn_resid.astype(jnp.float32)
    scale_row = lax.rsqrt(jnp.mean(resid_wide * resid_wide, axis=-1, keepdims=True) + norm_eps)
    normed = (resid_wide * scale_row * norm_gain).astype(jnp.bfloat16)
    gate_rows = route_gates[0]
    shares = gate_rows / jnp.sum(gate_rows, axis=-1, keepdims=True)
    hits = route_ids[0][:, :, None] == jnp.arange(EXPERTS, dtype=jnp.int32)[None, None, :]
    dense = jnp.sum(jnp.where(hits, shares[:, :, None], 0.0), axis=1)
    wanted = jnp.pad(dense.T.reshape(exp_count, 2, token_rows), ((0, 0), (0, 6), (0, 0)))
    shares_here = lax.all_to_all(wanted, "exp", split_axis=0, concat_axis=0, tiled=True)
    layer_out = moe(normed, attn_resid, shares_here, expert_gate, expert_up, expert_down)
    return (attn_resid[None], layer_out[None])


def solution(mesh):
    in_specs = (
        P("exp", "ctx", None),
        P("exp", "ctx", None),
        P("exp", "ctx", None),
        P("exp", "ctx", None),
        P("ctx", "exp"),
        P(),
        P("exp", None, None),
        P("exp", None, None),
        P("exp", None, None),
        P("exp", "ctx", None),
        P("exp", "ctx", None),
    )
    out_specs = (P("exp", "ctx", None), P("exp", "ctx", None))
    return jax.shard_map(local, mesh=mesh, in_specs=in_specs, out_specs=out_specs, check_vma=False)
```

```python
import functools

import jax
import jax.numpy as jnp
from jax import lax
from jax.experimental import pallas as pl
from jax.experimental.pallas import tpu as pltpu
from jax.sharding import PartitionSpec as P

QUERY_HEAD_COUNT = 32
KEY_VALUE_HEADS = 4
HEAD_SIZE = 128
TOPK = 8
CAP = 64
TOK = 128
D = 2048
FF = 768
EXPERTS = 32
MESH = pl.DeviceIdType.MESH

norm_eps = 1e-06
mask_fill_value = -1e30

RELATIONS = ((0, 0), (3, 0), (1, 0), (0, 1), (2, 0), (3, 1), (1, 1), (2, 1))
PAIRS = ((0, 3), (1, 2), (4, 7), (5, 6))


def moe_kernel(
    normed_ref,
    resid_ref,
    share_ref,
    gate_hbm,
    up_hbm,
    down_hbm,
    out_ref,
    gate_w,
    up_w,
    down_w,
    blocks,
    parts,
    sib_parts,
    half_in,
    full_in,
    far_in,
    hop_in,
    slots_in,
    slots_out,
    act,
    weight_sem,
    ag_send,
    ag_recv,
    sib_send,
    sib_recv,
    part_send,
    part_recv,
    rs_send,
    rs_recv,
):
    me = lax.axis_index("exp")
    z, xh, core = me // 4, lax.rem(me // 2, 2), lax.rem(me, 2)

    def block_of(relation, which):
        dz, dx = RELATIONS[relation]
        return lax.rem(z + dz, 4) * 4 + lax.rem(xh + dx, 2) * 2 + which

    other = 1 - core
    sibling = me + 1 - 2 * core
    z_up, z_down, x_over = block_of(2, core), block_of(1, core), block_of(3, core)

    loads = []
    for number, (src, dst) in enumerate(((gate_hbm, gate_w), (up_hbm, up_w), (down_hbm, down_w))):
        loads.append(pltpu.make_async_copy(src, dst, weight_sem.at[number]))
        loads[-1].start()
    blocks[me] = normed_ref[...]

    barrier = pltpu.get_barrier_semaphore()
    for peer in (sibling, z_up, z_down, x_over):
        pl.semaphore_signal(barrier, inc=1, device_id={"exp": peer}, device_id_type=MESH)
    pl.semaphore_wait(barrier, 4)

    def send(src, dst, sems, number, peer):
        return pltpu.make_async_remote_copy(
            src_ref=src,
            dst_ref=dst,
            send_sem=sems[0].at[number],
            recv_sem=sems[1].at[number],
            device_id={"exp": peer},
            device_id_type=MESH,
        )

    ag = (ag_send, ag_recv)
    sib = (sib_send, sib_recv)
    part = (part_send, part_recv)
    rs = (rs_send, rs_recv)
    low, high = pl.ds(0, CAP), pl.ds(CAP, CAP)

    def whole(relation):
        return blocks.at[block_of(relation, core)]

    def half(relation, rows):
        return blocks.at[block_of(relation, core), rows]

    ag_out = (
        send(whole(0), whole(0), ag, 0, z_up),
        send(whole(0), whole(0), ag, 1, z_down),
        send(whole(0), whole(0), ag, 2, x_over),
        send(half(1, low), half(1, low), ag, 3, z_up),
        send(half(2, high), half(2, high), ag, 4, z_down),
        send(whole(3), whole(3), ag, 5, z_up),
        send(whole(3), whole(3), ag, 6, z_down),
        send(whole(4), whole(4), ag, 7, x_over),
    )
    ag_in = (
        send(whole(1), whole(1), ag, 0, z_up),
        send(whole(2), whole(2), ag, 1, z_down),
        send(whole(3), whole(3), ag, 2, x_over),
        send(half(4, low), half(4, low), ag, 3, z_up),
        send(half(4, high), half(4, high), ag, 4, z_down),
        send(whole(5), whole(5), ag, 5, z_up),
        send(whole(6), whole(6), ag, 6, z_down),
        send(whole(7), whole(7), ag, 7, x_over),
    )
    sib_out = [send(whole(k), whole(k), sib, k, sibling) for k in range(8)]
    sib_in = []
    for k in range(8):
        arriving = blocks.at[block_of(k, other)]
        sib_in.append(send(arriving, arriving, sib, k, sibling))

    for number in (0, 1, 2):
        ag_out[number].start()
    sib_out[0].start()
    for load in loads:
        load.wait()

    lane = lax.broadcasted_iota(jnp.int32, (TOK, TOK), 1)
    row = lax.broadcasted_iota(jnp.int32, (TOK, TOK), 0)
    up_to = (row <= lane).astype(jnp.bfloat16)
    slot_of_row = lax.rem(row, CAP).astype(jnp.float32)

    def part_copy(chip):
        return send(parts.at[chip * 2 + other], sib_parts.at[chip], part, chip, sibling)

    first_row = lax.rem(me, 4) * 2

    def selection(block):
        share_rows = jnp.concatenate(
            [
                jnp.broadcast_to(share_ref[block, pl.ds(first_row + j, 1)], (CAP, TOK))
                for j in range(2)
            ],
            axis=0,
        )
        chosen = share_rows > 0.0
        count = jnp.dot(
            chosen.astype(jnp.float32).astype(jnp.bfloat16),
            up_to,
            preferred_element_type=jnp.float32,
        )
        picked = chosen & (count - 1.0 == slot_of_row)
        slot_share = jnp.sum(jnp.where(picked, share_rows, 0.0), axis=1, keepdims=True)
        return picked.astype(jnp.float32), slot_share

    def step(number, carry):
        @pl.when(number == 0)
        def _():
            ag_in[0].wait_recv()
            ag_out[3].start()
            sib_out[1].start()
            ag_in[1].wait_recv()
            ag_out[4].start()
            sib_out[2].start()
            ag_in[2].wait_recv()
            ag_out[5].start()
            ag_out[6].start()
            sib_out[3].start()
            sib_in[0].wait_recv()
            sib_in[3].wait_recv()

        @pl.when(number == 1)
        def _():
            ag_in[3].wait_recv()
            ag_in[4].wait_recv()
            ag_out[7].start()
            sib_out[4].start()
            sib_in[1].wait_recv()
            sib_in[2].wait_recv()

        @pl.when(number == 2)
        def _():
            ag_in[5].wait_recv()
            sib_out[5].start()
            ag_in[6].wait_recv()
            sib_out[6].start()
            ag_in[7].wait_recv()
            sib_out[7].start()
            sib_in[4].wait_recv()
            sib_in[7].wait_recv()

        @pl.when(number == 3)
        def _():
            sib_in[5].wait_recv()
            sib_in[6].wait_recv()

        def chip_at(which):
            dz, dx = 0, 0
            for k, pair in enumerate(PAIRS):
                here = RELATIONS[pair[which]]
                dz = jnp.where(number == k, here[0], dz)
                dx = jnp.where(number == k, here[1], dx)
            return lax.rem(z + dz, 4) * 2 + lax.rem(xh + dx, 2)

        chips = (chip_at(0), chip_at(1))
        sources = [chips[q // 2] * 2 + q % 2 for q in range(4)]
        for q in range(4):
            picked, _ = selection(sources[q])
            found = jnp.dot(
                picked.astype(jnp.bfloat16),
                blocks[sources[q]],
                preferred_element_type=jnp.float32,
            ).astype(jnp.bfloat16)
            for j in range(2):
                slots_in[j, q * CAP : (q + 1) * CAP] = found[j * CAP : (j + 1) * CAP]

        def expert(j, carry):
            for n in range(3):
                cols = slice(n * 256, (n + 1) * 256)
                gate_part = jnp.dot(
                    slots_in[j], gate_w[j, :, cols], preferred_element_type=jnp.float32
                )
                up_part = jnp.dot(
                    slots_in[j], up_w[j, :, cols], preferred_element_type=jnp.float32
                )
                act[:, cols] = (gate_part / (1.0 + jnp.exp(-gate_part)) * up_part).astype(
                    jnp.bfloat16
                )
            for n in range(4):
                cols = slice(n * 512, (n + 1) * 512)
                result = jnp.dot(act[...], down_w[j, :, cols], preferred_element_type=jnp.float32)
                for q in range(4):
                    slots_out[q, pl.ds(pl.multiple_of(j * CAP, CAP), CAP), cols] = result[
                        q * CAP : (q + 1) * CAP
                    ].astype(jnp.bfloat16)
            return carry

        lax.fori_loop(0, 2, expert, 0)
        for q in range(4):
            picked, slot_share = selection(sources[q])
            scaled = (slots_out[q].astype(jnp.float32) * slot_share).astype(jnp.bfloat16)
            parts[sources[q]] = jnp.dot(
                picked.T.astype(jnp.bfloat16), scaled, preferred_element_type=jnp.float32
            ).astype(jnp.bfloat16)
            if q % 2:
                part_copy(chips[q // 2]).start()
        return carry

    lax.fori_loop(0, 4, step, 0)

    def chip_sum(relation):
        dz, dx = RELATIONS[relation]
        chip = lax.rem(z + dz, 4) * 2 + lax.rem(xh + dx, 2)
        pltpu.make_async_remote_copy(
            src_ref=parts.at[chip * 2 + other],
            dst_ref=sib_parts.at[chip],
            send_sem=part_send.at[chip],
            recv_sem=part_recv.at[chip],
            device_id={"exp": sibling},
            device_id_type=MESH,
        ).wait_recv()
        add_into(chip * 2 + core, slice(None), sib_parts.at[chip])

    def add_into(block, rows, extra):
        parts[block, rows] = (
            parts[block, rows].astype(jnp.float32) + extra[...].astype(jnp.float32)
        ).astype(jnp.bfloat16)

    def part_of(relation):
        return parts.at[block_of(relation, core)]

    chip_sum(7)
    rs_out = [send(part_of(7), hop_in, rs, 0, x_over)]
    rs_out[0].start()
    chip_sum(5)
    rs_out.append(send(part_of(5), full_in.at[2], rs, 1, z_down))
    rs_out[1].start()
    chip_sum(6)
    rs_out.append(send(part_of(6), full_in.at[3], rs, 2, z_up))
    rs_out[2].start()
    chip_sum(4)
    rs_out[0].wait_recv()
    add_into(block_of(4, core), slice(None), hop_in)
    rs_out.append(
        send(parts.at[block_of(4, core), low], half_in.at[0], rs, 3, z_down)
    )
    rs_out[3].start()
    rs_out.append(send(parts.at[block_of(4, core), high], half_in.at[1], rs, 4, z_up))
    rs_out[4].start()
    chip_sum(3)
    chip_sum(1)
    chip_sum(2)
    chip_sum(0)
    rs_out[1].wait_recv()
    add_into(block_of(3, core), slice(None), full_in.at[2])
    rs_out[2].wait_recv()
    add_into(block_of(3, core), slice(None), full_in.at[3])
    rs_out.append(send(part_of(3), far_in, rs, 5, x_over))
    rs_out[5].start()
    rs_out[3].wait_recv()
    add_into(block_of(1, core), slice(0, CAP), half_in.at[0])
    rs_out.append(send(part_of(1), full_in.at[0], rs, 6, z_down))
    rs_out[6].start()
    rs_out[4].wait_recv()
    add_into(block_of(2, core), slice(CAP, TOK), half_in.at[1])
    rs_out.append(send(part_of(2), full_in.at[1], rs, 7, z_up))
    rs_out[7].start()

    rs_out[6].wait_recv()
    rs_out[7].wait_recv()
    rs_out[5].wait_recv()
    total = resid_ref[...].astype(jnp.float32) + parts[me].astype(jnp.float32)
    for extra in (full_in.at[0], full_in.at[1], far_in):
        total = total + extra[...].astype(jnp.float32)
    out_ref[...] = total.astype(jnp.bfloat16)

    for copy in (*ag_out, *sib_out, *rs_out):
        copy.wait_send()
    for chip in range(8):
        part_copy(chip).wait_send()


def moe(normed, attn_resid, shares, expert_gate, expert_up, expert_down):
    vmem = pl.BlockSpec(memory_space=pltpu.VMEM)
    hbm = pl.BlockSpec(memory_space=pl.ANY)
    dma = pltpu.SemaphoreType.DMA
    bf16 = jnp.bfloat16
    return pl.pallas_call(
        moe_kernel,
        out_shape=jax.ShapeDtypeStruct((TOK, D), bf16),
        in_specs=[vmem, vmem, vmem, hbm, hbm, hbm],
        out_specs=vmem,
        scratch_shapes=[
            pltpu.VMEM((2, D, FF), bf16),
            pltpu.VMEM((2, D, FF), bf16),
            pltpu.VMEM((2, FF, D), bf16),
            pltpu.VMEM((16, TOK, D), bf16),
            pltpu.VMEM((16, TOK, D), bf16),
            pltpu.VMEM((8, TOK, D), bf16),
            pltpu.VMEM((2, CAP, D), bf16),
            pltpu.VMEM((4, TOK, D), bf16),
            pltpu.VMEM((TOK, D), bf16),
            pltpu.VMEM((TOK, D), bf16),
            pltpu.VMEM((2, 256, D), bf16),
            pltpu.VMEM((4, TOK, D), bf16),
            pltpu.VMEM((256, FF), bf16),
            dma((3,)),
            dma((8,)),
            dma((8,)),
            dma((8,)),
            dma((8,)),
            dma((8,)),
            dma((8,)),
            dma((8,)),
            dma((8,)),
        ],
        compiler_params=pltpu.CompilerParams(
            collective_id=1, has_side_effects=True, vmem_limit_bytes=60 << 20
        ),
    )(normed, attn_resid, shares, expert_gate, expert_up, expert_down)


def from_behind(shard, axis, by):
    devices = lax.axis_size(axis)
    pairs = [(i, i + by) for i in range(devices) if 0 <= i + by < devices]
    return lax.ppermute(shard, axis, pairs)


PIECES = ((0, 224, "xyz"), (224, 160, "yzx"), (384, 128, "zxy"))


def front_kernel(
    queries_ref,
    keys_ref,
    values_ref,
    resid_ref,
    weight_ref,
    gain_ref,
    ids_ref,
    gates_ref,
    normed_ref,
    attn_resid_ref,
    shares_ref,
    weight,
    kv,
    stacked,
    attended,
    to_sibling,
    from_sibling,
    share_tiles,
    shares_in,
    kv_send,
    kv_recv,
    w_send,
    w_recv,
    share_send,
    share_recv,
    att_send,
    att_recv,
    proj_send,
    proj_recv,
):
    ctx, exp = lax.axis_index("ctx"), lax.axis_index("exp")
    x_low, y = ctx // 4, lax.rem(ctx, 4)
    z, x_high, core = exp // 4, lax.rem(exp // 2, 2), lax.rem(exp, 2)
    here = {"x": x_high * 2 + x_low, "y": y, "z": z}
    other = 1 - core
    sibling = {"ctx": ctx, "exp": exp + 1 - 2 * core}

    def device(x, y_at, z_at):
        return {"ctx": lax.rem(x, 2) * 4 + y_at, "exp": z_at * 4 + (x // 2) * 2 + core}

    def neighbour(axis, by):
        there = dict(here)
        there[axis] = lax.rem(here[axis] + by, 4)
        return device(there["x"], there["y"], there["z"])

    partner = {"ctx": (1 - x_low) * 4 + y, "exp": exp}

    def send(src, dst, sems, number, peer):
        return pltpu.make_async_remote_copy(
            src_ref=src,
            dst_ref=dst,
            send_sem=sems[0].at[number],
            recv_sem=sems[1].at[number],
            device_id=peer,
            device_id_type=MESH,
        )

    kv[ctx, 0] = keys_ref[...]
    kv[ctx, 1] = values_ref[...]
    weight[x_high, x_low, y, :, pl.ds(pl.multiple_of(z * 128, 128), 128)] = weight_ref[...]

    barrier = pltpu.get_barrier_semaphore()
    for step in range(1, 16):
        pl.semaphore_signal(
            barrier,
            inc=1,
            device_id={"ctx": ctx, "exp": lax.rem(exp + step, 16)},
            device_id_type=MESH,
        )
    for axis in ("x", "y"):
        for by in (1, 3):
            pl.semaphore_signal(
                barrier, inc=1, device_id=neighbour(axis, by), device_id_type=MESH
            )
    pl.semaphore_wait(barrier, 19)

    kv_sems = (kv_send, kv_recv)

    def kv_block(dy, dx):
        return lax.rem(x_low + dx, 2) * 4 + lax.rem(y + dy, 4)

    y_up, y_down = neighbour("y", 1), neighbour("y", 3)

    def kv_copy(number, block, part, peer):
        ref = kv.at[block] if part is None else kv.at[block, part]
        return send(ref, ref, kv_sems, number, peer)

    kv_out = (
        kv_copy(0, kv_block(0, 0), None, y_up),
        kv_copy(1, kv_block(0, 0), None, y_down),
        kv_copy(2, kv_block(0, 0), None, partner),
        kv_copy(3, kv_block(3, 0), 0, y_up),
        kv_copy(4, kv_block(1, 0), 1, y_down),
        kv_copy(5, kv_block(0, 1), None, y_up),
        kv_copy(6, kv_block(0, 1), None, y_down),
        kv_copy(7, kv_block(2, 0), None, partner),
    )
    kv_in = (
        kv_copy(0, kv_block(3, 0), None, y_up),
        kv_copy(1, kv_block(1, 0), None, y_down),
        kv_copy(2, kv_block(0, 1), None, partner),
        kv_copy(3, kv_block(2, 0), 0, y_up),
        kv_copy(4, kv_block(2, 0), 1, y_down),
        kv_copy(5, kv_block(3, 1), None, y_up),
        kv_copy(6, kv_block(1, 1), None, y_down),
        kv_copy(7, kv_block(2, 1), None, partner),
    )

    w_sems = (w_send, w_recv)

    def segment(piece, stage, by, rows):
        order = PIECES[piece][2]
        at = {}
        for axis in order[stage:]:
            at[axis] = here[axis]
        at[order[stage]] = lax.rem(here[order[stage]] + by, 4)
        full = slice(None)
        lanes = pl.ds(pl.multiple_of(at["z"] * 128, 128), 128) if "z" in at else full
        x_pair = (at["x"] // 2, lax.rem(at["x"], 2)) if "x" in at else (full, full)
        return weight.at[x_pair[0], x_pair[1], at.get("y", full), rows, lanes]

    def w_copies(piece, stage):
        first, height, order = PIECES[piece]
        whole = pl.ds(first, height)
        halves = (pl.ds(first, height // 2), pl.ds(first + height // 2, height // 2))
        axis = order[stage]
        up, down = neighbour(axis, 1), neighbour(axis, 3)
        base = (piece * 3 + stage) * 4
        out, arrive = [], []
        for number, (sent, got, rows, peer) in enumerate(
            (
                (0, 3, whole, up),
                (0, 1, whole, down),
                (3, 2, halves[0], up),
                (1, 2, halves[1], down),
            )
        ):
            mine = segment(piece, stage, sent, rows)
            theirs = segment(piece, stage, got, rows)
            out.append(send(mine, mine, w_sems, base + number, peer))
            arrive.append(send(theirs, theirs, w_sems, base + number, peer))
        return out, arrive

    w_plan = [[w_copies(piece, stage) for stage in range(3)] for piece in range(3)]

    def w_begin(stage):
        for piece in range(3):
            for number in (0, 1):
                w_plan[piece][stage][0][number].start()

    def w_forward(stage):
        for piece in range(3):
            out, arrive = w_plan[piece][stage]
            for number in (0, 1):
                arrive[number].wait_recv()
                out[number + 2].start()

    def w_end(stage):
        for piece in range(3):
            for number in (2, 3):
                w_plan[piece][stage][1][number].wait_recv()

    for number in (0, 1, 2):
        kv_out[number].start()
    w_begin(0)

    gates = gates_ref[...]
    shares = gates / jnp.sum(gates, axis=1, keepdims=True)
    ids = ids_ref[...]
    lane = lax.broadcasted_iota(jnp.int32, (TOK, TOK), 1)
    dense = jnp.zeros((TOK, TOK), jnp.float32)
    for k in range(TOPK):
        dense = dense + jnp.where(ids[:, k : k + 1] == lane, shares[:, k : k + 1], 0.0)
    flipped = dense.T
    for group in range(4):
        share_tiles[group] = flipped[group * 8 : (group + 1) * 8]
    shares_in[exp] = share_tiles[exp // 4]
    share_sems = (share_send, share_recv)
    share_out, share_arrive = [], []
    for step in range(1, 16):
        there = lax.rem(exp + step, 16)
        share_out.append(
            send(
                share_tiles.at[there // 4],
                shares_in.at[exp],
                share_sems,
                step,
                {"ctx": ctx, "exp": there},
            )
        )
        behind = lax.rem(exp + 16 - step, 16)
        share_arrive.append(
            send(
                share_tiles.at[there // 4],
                shares_in.at[behind],
                share_sems,
                step,
                {"ctx": ctx, "exp": there},
            )
        )
        share_out[-1].start()

    w_forward(0)
    for head in range(QUERY_HEAD_COUNT):
        stacked[head // 4, (head % 4) * TOK : (head % 4 + 1) * TOK] = queries_ref[
            :, head * HEAD_SIZE : (head + 1) * HEAD_SIZE
        ]
    w_end(0)
    w_begin(1)
    for number in (0, 1, 2):
        kv_in[number].wait_recv()
    for number in (3, 4, 5, 6):
        kv_out[number].start()
    w_forward(1)
    kv_in[3].wait_recv()
    kv_in[4].wait_recv()
    kv_out[7].start()
    w_end(1)
    w_begin(2)
    for number in (5, 6, 7):
        kv_in[number].wait_recv()

    att_sems = (att_send, att_recv)

    def att_copy(number):
        part = attended.at[core, :, pl.ds(pl.multiple_of(number * 512, 512), 512)]
        return send(part, part, att_sems, number, sibling)

    keys_total = 8 * TOK
    scale = HEAD_SIZE**-0.5 * 1.4426950408889634

    def heads(quad, carry):
        lanes = pl.ds(pl.multiple_of((quad // 2) * HEAD_SIZE, HEAD_SIZE), HEAD_SIZE)
        keys_here = jnp.concatenate([kv[block, 0, :, lanes] for block in range(8)], axis=0)
        values_here = jnp.concatenate([kv[block, 1, :, lanes] for block in range(8)], axis=0)
        values_wide = jnp.concatenate([values_here, jnp.ones_like(values_here)], axis=1)
        for part in range(4):
            scores = lax.dot_general(
                stacked[quad, part * TOK : (part + 1) * TOK],
                keys_here,
                (((1,), (1,)), ((), ())),
                preferred_element_type=jnp.float32,
            )
            query_at = lax.broadcasted_iota(jnp.int32, (TOK, keys_total), 0) + ctx * TOK
            key_at = lax.broadcasted_iota(jnp.int32, (TOK, keys_total), 1)
            scores = jnp.where(query_at >= key_at, scores, mask_fill_value)
            top = jnp.max(scores, axis=1, keepdims=True)
            weights = jnp.exp2((scores - top) * scale).astype(jnp.bfloat16)
            result = jnp.dot(weights, values_wide, preferred_element_type=jnp.float32)
            attended[
                core,
                :,
                pl.ds(pl.multiple_of(quad * 512 + part * HEAD_SIZE, HEAD_SIZE), HEAD_SIZE),
            ] = (result[:, :HEAD_SIZE] / result[:, HEAD_SIZE:]).astype(jnp.bfloat16)
        att_copy(quad).start()
        return carry

    lax.fori_loop(0, 8, heads, 0)
    w_forward(2)
    for number in range(8):
        part = attended.at[other, :, pl.ds(number * 512, 512)]
        send(part, part, att_sems, number, sibling).wait_recv()
    w_end(2)

    def project(half, carry):
        rows = weight[half].reshape(8 * 512, 512)
        mine = jnp.dot(attended[core], rows, preferred_element_type=jnp.float32)
        theirs = jnp.dot(attended[other], rows, preferred_element_type=jnp.float32)
        to_sibling[half] = theirs
        from_sibling[2 + half] = mine
        return carry

    lax.fori_loop(0, 2, project, 0)
    swap = send(to_sibling, from_sibling.at[pl.ds(0, 2)], (proj_send, proj_recv), 0, sibling)
    swap.start()

    def place(first, which):
        for half in range(2):
            for depth in range(4):
                lanes = pl.ds(
                    pl.multiple_of(depth * 512 + half * 256 + which * 128, 128), 128
                )
                attn_resid_ref[:, lanes] = (
                    resid_ref[:, lanes].astype(jnp.float32)
                    + from_sibling[first + half, :, depth * 128 : (depth + 1) * 128]
                ).astype(jnp.bfloat16)

    place(2, core)
    for arriving in share_arrive:
        arriving.wait_recv()
    shares_ref[...] = shares_in[...]
    swap.wait_recv()
    place(0, other)
    wide = attn_resid_ref[...].astype(jnp.float32)
    scale_row = lax.rsqrt(jnp.mean(wide * wide, axis=1, keepdims=True) + norm_eps)
    normed_ref[...] = (wide * scale_row * gain_ref[...]).astype(jnp.bfloat16)

    for copy in (*kv_out, *share_out):
        copy.wait_send()
    for piece in range(3):
        for stage in range(3):
            for copy in w_plan[piece][stage][0]:
                copy.wait_send()
    for number in range(8):
        att_copy(number).wait_send()
    swap.wait_send()


def front(queries, keys, values, resid, out_weight, norm_gain, route_ids, route_gates):
    vmem = pl.BlockSpec(memory_space=pltpu.VMEM)
    dma = pltpu.SemaphoreType.DMA
    bf16, f32 = jnp.bfloat16, jnp.float32
    return pl.pallas_call(
        front_kernel,
        out_shape=(
            jax.ShapeDtypeStruct((TOK, D), bf16),
            jax.ShapeDtypeStruct((TOK, D), bf16),
            jax.ShapeDtypeStruct((16, 8, TOK), f32),
        ),
        in_specs=[vmem] * 8,
        out_specs=(vmem, vmem, vmem),
        scratch_shapes=[
            pltpu.VMEM((2, 2, 4, 512, 512), bf16),
            pltpu.VMEM((8, 2, TOK, 512), bf16),
            pltpu.VMEM((8, 512, HEAD_SIZE), bf16),
            pltpu.VMEM((2, TOK, 4096), bf16),
            pltpu.VMEM((2, TOK, 512), f32),
            pltpu.VMEM((4, TOK, 512), f32),
            pltpu.VMEM((4, 8, TOK), f32),
            pltpu.VMEM((16, 8, TOK), f32),
            dma((8,)),
            dma((8,)),
            dma((36,)),
            dma((36,)),
            dma((16,)),
            dma((16,)),
            dma((8,)),
            dma((8,)),
            dma((1,)),
            dma((1,)),
        ],
        compiler_params=pltpu.CompilerParams(
            collective_id=0, has_side_effects=True, vmem_limit_bytes=40 << 20
        ),
    )(queries, keys, values, resid, out_weight, norm_gain, route_ids, route_gates)


def local(
    queries,
    keys,
    values,
    resid,
    out_weight,
    norm_gain,
    expert_gate,
    expert_up,
    expert_down,
    route_ids,
    route_gates,
):
    normed, attn_resid, shares = front(
        queries[0],
        keys[0],
        values[0],
        resid[0],
        out_weight,
        norm_gain[None],
        route_ids[0],
        route_gates[0],
    )
    layer_out = moe(normed, attn_resid, shares, expert_gate, expert_up, expert_down)
    return (attn_resid[None], layer_out[None])


def solution(mesh):
    in_specs = (
        P("exp", "ctx", None),
        P("exp", "ctx", None),
        P("exp", "ctx", None),
        P("exp", "ctx", None),
        P("ctx", "exp"),
        P(),
        P("exp", None, None),
        P("exp", None, None),
        P("exp", None, None),
        P("exp", "ctx", None),
        P("exp", "ctx", None),
    )
    out_specs = (P("exp", "ctx", None), P("exp", "ctx", None))
    return jax.shard_map(local, mesh=mesh, in_specs=in_specs, out_specs=out_specs, check_vma=False)
```

```python
import functools

import jax
import jax.numpy as jnp
from jax import lax
from jax.experimental import pallas as pl
from jax.experimental.pallas import tpu as pltpu
from jax.sharding import PartitionSpec as P

QUERY_HEAD_COUNT = 32
HEAD_SIZE = 128
TOPK = 8
CAP = 64
TOK = 128
D = 2048
FF = 768
EXPERTS = 32
MESH = pl.DeviceIdType.MESH

norm_eps = 1e-06
mask_fill_value = -1e30

RELATIONS = ((0, 0), (3, 0), (1, 0), (0, 1), (2, 0), (3, 1), (1, 1), (2, 1))
PAIRS = ((0, 3), (1, 2), (4, 7), (5, 6))
PIECES = ((0, 208, 112, "xyz"), (208, 160, 80, "yzx"), (368, 144, 80, "zxy"))


def layer_kernel(
    queries_hbm,
    keys_hbm,
    values_hbm,
    resid_hbm,
    weight_hbm,
    gain_hbm,
    ids_hbm,
    gates_hbm,
    gate_hbm,
    up_hbm,
    down_hbm,
    attn_resid_ref,
    out_ref,
    weight,
    kv,
    stacked,
    attended,
    to_sibling,
    from_sibling,
    resid,
    gain,
    ids,
    gates,
    share_tiles,
    shares_in,
    gate_w,
    up_w,
    down_w,
    blocks,
    sib_parts,
    half_in,
    full_in,
    far_in,
    hop_in,
    slots_in,
    slots_out,
    act,
    pick,
    scatter,
    load_sem,
    query_sem,
    expert_sem,
    kv_send,
    kv_recv,
    w_send,
    w_recv,
    share_send,
    share_recv,
    att_send,
    att_recv,
    proj_send,
    proj_recv,
    ag_send,
    ag_recv,
    sib_send,
    sib_recv,
    part_send,
    part_recv,
    rs_send,
    rs_recv,
):
    ctx, exp = lax.axis_index("ctx"), lax.axis_index("exp")
    x_low, y = ctx // 4, lax.rem(ctx, 4)
    z, x_high, core = exp // 4, lax.rem(exp // 2, 2), lax.rem(exp, 2)
    here = {"x": x_high * 2 + x_low, "y": y, "z": z}
    other = 1 - core

    def device(x, y_at, z_at):
        return {"ctx": lax.rem(x, 2) * 4 + y_at, "exp": z_at * 4 + (x // 2) * 2 + core}

    def neighbour(axis, by):
        there = dict(here)
        there[axis] = lax.rem(here[axis] + by, 4)
        return device(there["x"], there["y"], there["z"])

    sibling = {"ctx": ctx, "exp": exp + 1 - 2 * core}
    partner = {"ctx": (1 - x_low) * 4 + y, "exp": exp}
    y_up, y_down = neighbour("y", 1), neighbour("y", 3)
    z_up, z_down, x_over = neighbour("z", 1), neighbour("z", 3), neighbour("x", 2)

    def send(src, dst, sems, number, peer):
        return pltpu.make_async_remote_copy(
            src_ref=src,
            dst_ref=dst,
            send_sem=sems[0].at[number],
            recv_sem=sems[1].at[number],
            device_id=peer,
            device_id_type=MESH,
        )

    own_weight = weight.at[
        x_high, x_low, y, :, pl.ds(pl.multiple_of(z * 128, 128), 128)
    ]
    loads = []
    for number, (src, dst) in enumerate(
        (
            (weight_hbm, own_weight),
            (keys_hbm, kv.at[ctx, 0]),
            (values_hbm, kv.at[ctx, 1]),
            (ids_hbm, ids),
            (gates_hbm, gates),
            (gain_hbm, gain),
            (resid_hbm, resid),
        )
    ):
        loads.append(pltpu.make_async_copy(src, dst, load_sem.at[number]))
        loads[-1].start()
    query_loads = []
    for head in range(QUERY_HEAD_COUNT):
        query_loads.append(
            pltpu.make_async_copy(
                queries_hbm.at[:, pl.ds(head * HEAD_SIZE, HEAD_SIZE)],
                stacked.at[head // 4, pl.ds((head % 4) * TOK, TOK)],
                query_sem.at[head],
            )
        )
        query_loads[-1].start()

    barrier = pltpu.get_barrier_semaphore()
    for step in range(1, 16):
        pl.semaphore_signal(
            barrier,
            inc=1,
            device_id={"ctx": ctx, "exp": lax.rem(exp + step, 16)},
            device_id_type=MESH,
        )
    for by in (1, 2, 3):
        pl.semaphore_signal(barrier, inc=1, device_id=neighbour("y", by), device_id_type=MESH)
    for by in (1, 3):
        pl.semaphore_signal(barrier, inc=1, device_id=neighbour("x", by), device_id_type=MESH)
    pl.semaphore_wait(barrier, 20)

    w_sems = (w_send, w_recv)

    def segment(piece, stage, by, rows):
        order = PIECES[piece][3]
        at = {}
        for axis in order[stage:]:
            at[axis] = here[axis]
        at[order[stage]] = lax.rem(here[order[stage]] + by, 4)
        full = slice(None)
        lanes = pl.ds(pl.multiple_of(at["z"] * 128, 128), 128) if "z" in at else full
        x_pair = (at["x"] // 2, lax.rem(at["x"], 2)) if "x" in at else (full, full)
        return weight.at[x_pair[0], x_pair[1], at.get("y", full), rows, lanes]

    def w_copies(piece, stage):
        first, height, cut, order = PIECES[piece]
        axis = order[stage]
        whole = pl.ds(first, height)
        top, bottom = pl.ds(first, cut), pl.ds(first + cut, height - cut)
        if stage < 2:
            base = piece * 12 + stage * 3
            moves = [(0, 4 - by, whole, neighbour(axis, by)) for by in (1, 3, 2)]
        else:
            base = piece * 12 + 6
            up, down = neighbour(axis, 1), neighbour(axis, 3)
            moves = [
                (0, 3, top, up),
                (0, 1, bottom, down),
                (0, 3, bottom, up),
                (0, 1, top, down),
                (3, 2, top, up),
                (1, 2, bottom, down),
            ]
        out, arrive = [], []
        for number, (sent, got, rows, peer) in enumerate(moves):
            mine = segment(piece, stage, sent, rows)
            theirs = segment(piece, stage, got, rows)
            out.append(send(mine, mine, w_sems, base + number, peer))
            arrive.append(send(theirs, theirs, w_sems, base + number, peer))
        return out, arrive

    w_plan = [[w_copies(piece, stage) for stage in range(3)] for piece in range(3)]

    def w_begin(stage):
        for number in range(3 if stage < 2 else 4):
            for piece in range(3):
                w_plan[piece][stage][0][number].start()

    def w_end(stage):
        for piece in range(3):
            for number in (0, 1, 2) if stage < 2 else (2, 3, 4, 5):
                w_plan[piece][stage][1][number].wait_recv()

    def w_forward(piece):
        out, arrive = w_plan[piece][2]
        arrive[0].wait_recv()
        out[4].start()
        arrive[1].wait_recv()
        out[5].start()

    kv_sems = (kv_send, kv_recv)

    def kv_block(dy, dx):
        return lax.rem(x_low + dx, 2) * 4 + lax.rem(y + dy, 4)

    def kv_copy(number, block, part, peer):
        ref = kv.at[block] if part is None else kv.at[block, part]
        return send(ref, ref, kv_sems, number, peer)

    kv_out = (
        kv_copy(0, kv_block(0, 0), None, y_up),
        kv_copy(1, kv_block(0, 0), None, y_down),
        kv_copy(2, kv_block(0, 0), None, partner),
        kv_copy(3, kv_block(3, 0), 0, y_up),
        kv_copy(4, kv_block(1, 0), 1, y_down),
        kv_copy(5, kv_block(0, 1), None, y_up),
        kv_copy(6, kv_block(0, 1), None, y_down),
        kv_copy(7, kv_block(2, 0), None, partner),
    )
    kv_in = (
        kv_copy(0, kv_block(3, 0), None, y_up),
        kv_copy(1, kv_block(1, 0), None, y_down),
        kv_copy(2, kv_block(0, 1), None, partner),
        kv_copy(3, kv_block(2, 0), 0, y_up),
        kv_copy(4, kv_block(2, 0), 1, y_down),
        kv_copy(5, kv_block(3, 1), None, y_up),
        kv_copy(6, kv_block(1, 1), None, y_down),
        kv_copy(7, kv_block(2, 1), None, partner),
    )

    loads[0].wait()
    w_begin(0)
    loads[1].wait()
    loads[2].wait()
    for number in (0, 1, 2):
        kv_out[number].start()
    expert_loads = []
    for number, (src, dst) in enumerate(((gate_hbm, gate_w), (up_hbm, up_w), (down_hbm, down_w))):
        expert_loads.append(pltpu.make_async_copy(src, dst, expert_sem.at[number]))
        expert_loads[-1].start()

    loads[3].wait()
    loads[4].wait()
    shares = gates[...] / jnp.sum(gates[...], axis=0, keepdims=True)
    ids_here = ids[...]
    expert_row = lax.broadcasted_iota(jnp.int32, (EXPERTS, TOK), 0)
    dense = jnp.zeros((EXPERTS, TOK), jnp.float32)
    for k in range(TOPK):
        dense = dense + jnp.where(ids_here[k : k + 1] == expert_row, shares[k : k + 1], 0.0)
    for group in range(4):
        share_tiles[group] = dense[group * 8 : (group + 1) * 8]
    shares_in[exp] = share_tiles[exp // 4]
    share_sems = (share_send, share_recv)
    share_out, share_arrive = [], []
    for step in range(1, 16):
        there = lax.rem(exp + step, 16)
        behind = lax.rem(exp + 16 - step, 16)
        peer = {"ctx": ctx, "exp": there}
        tile = share_tiles.at[there // 4]
        share_out.append(send(tile, shares_in.at[exp], share_sems, step, peer))
        share_arrive.append(send(tile, shares_in.at[behind], share_sems, step, peer))

    w_end(0)
    w_begin(1)
    for copy in share_out:
        copy.start()
    for number in (0, 1, 2):
        kv_in[number].wait_recv()
    w_end(1)
    w_begin(2)
    for number in (3, 4, 5, 6):
        kv_out[number].start()
    kv_in[3].wait_recv()
    kv_in[4].wait_recv()
    kv_out[7].start()
    w_forward(0)
    for number in (5, 6, 7):
        kv_in[number].wait_recv()
    for copy in query_loads:
        copy.wait()

    att_sems = (att_send, att_recv)

    def att_copy(number):
        part = attended.at[core, :, pl.ds(pl.multiple_of(number * 512, 512), 512)]
        return send(part, part, att_sems, number, sibling)

    keys_total = 8 * TOK
    scale = HEAD_SIZE**-0.5 * 1.4426950408889634

    def heads(quad, carry):
        @pl.when(quad == 1)
        def _():
            w_forward(1)

        @pl.when(quad == 3)
        def _():
            w_forward(2)

        lanes = pl.ds(pl.multiple_of((quad // 2) * HEAD_SIZE, HEAD_SIZE), HEAD_SIZE)
        keys_here = jnp.concatenate([kv[block, 0, :, lanes] for block in range(8)], axis=0)
        values_here = jnp.concatenate([kv[block, 1, :, lanes] for block in range(8)], axis=0)
        values_wide = jnp.concatenate([values_here, jnp.ones_like(values_here)], axis=1)
        for part in range(4):
            scores = lax.dot_general(
                stacked[quad, part * TOK : (part + 1) * TOK],
                keys_here,
                (((1,), (1,)), ((), ())),
                preferred_element_type=jnp.float32,
            )
            query_at = lax.broadcasted_iota(jnp.int32, (TOK, keys_total), 0) + ctx * TOK
            key_at = lax.broadcasted_iota(jnp.int32, (TOK, keys_total), 1)
            scores = jnp.where(query_at >= key_at, scores, mask_fill_value)
            top = jnp.max(scores, axis=1, keepdims=True)
            weights = jnp.exp2((scores - top) * scale).astype(jnp.bfloat16)
            result = jnp.dot(weights, values_wide, preferred_element_type=jnp.float32)
            attended[
                core,
                :,
                pl.ds(pl.multiple_of(quad * 512 + part * HEAD_SIZE, HEAD_SIZE), HEAD_SIZE),
            ] = (result[:, :HEAD_SIZE] / result[:, HEAD_SIZE:]).astype(jnp.bfloat16)
        att_copy(quad).start()
        return carry

    lax.fori_loop(0, 8, heads, 0)

    for arriving in share_arrive:
        arriving.wait_recv()
    lane = lax.broadcasted_iota(jnp.int32, (TOK, TOK), 1)
    row = lax.broadcasted_iota(jnp.int32, (TOK, TOK), 0)
    up_to = (row <= lane).astype(jnp.float32).astype(jnp.bfloat16)
    slot_of_row = lax.rem(row, CAP).astype(jnp.float32)
    first_row = lax.rem(exp, 4) * 2

    def selection(block, carry):
        share_rows = jnp.concatenate(
            [
                jnp.broadcast_to(shares_in[block, pl.ds(first_row + j, 1)], (CAP, TOK))
                for j in range(2)
            ],
            axis=0,
        )
        chosen = share_rows > 0.0
        count = jnp.dot(
            chosen.astype(jnp.float32).astype(jnp.bfloat16),
            up_to,
            preferred_element_type=jnp.float32,
        )
        picked = chosen & (count - 1.0 == slot_of_row)
        pick[block] = picked.astype(jnp.float32).astype(jnp.bfloat16)
        scatter[block] = jnp.where(picked, share_rows, 0.0).T.astype(jnp.bfloat16)
        return carry

    lax.fori_loop(0, 16, selection, 0)

    for number in range(8):
        part = attended.at[other, :, pl.ds(number * 512, 512)]
        send(part, part, att_sems, number, sibling).wait_recv()
    w_end(2)

    def project(half, carry):
        rows = weight[half].reshape(8 * 512, 512)
        to_sibling[half] = jnp.dot(attended[other], rows, preferred_element_type=jnp.float32)
        from_sibling[2 + half] = jnp.dot(
            attended[core], rows, preferred_element_type=jnp.float32
        )
        return carry

    lax.fori_loop(0, 2, project, 0)
    swap = send(to_sibling, from_sibling.at[pl.ds(0, 2)], (proj_send, proj_recv), 0, sibling)
    swap.start()
    loads[5].wait()
    loads[6].wait()

    def place(first, which):
        for half in range(2):
            for depth in range(4):
                lanes = pl.ds(
                    pl.multiple_of(depth * 512 + half * 256 + which * 128, 128), 128
                )
                attn_resid_ref[:, lanes] = (
                    resid[:, lanes].astype(jnp.float32)
                    + from_sibling[first + half, :, depth * 128 : (depth + 1) * 128]
                ).astype(jnp.bfloat16)

    place(2, core)
    swap.wait_recv()
    place(0, other)
    wide = attn_resid_ref[...].astype(jnp.float32)
    scale_row = lax.rsqrt(jnp.mean(wide * wide, axis=1, keepdims=True) + norm_eps)
    blocks[exp] = (wide * scale_row * gain[...]).astype(jnp.bfloat16)

    def block_of(relation, which):
        dz, dx = RELATIONS[relation]
        return lax.rem(z + dz, 4) * 4 + lax.rem(x_high + dx, 2) * 2 + which

    ag = (ag_send, ag_recv)
    sib = (sib_send, sib_recv)
    low, high = pl.ds(0, CAP), pl.ds(CAP, CAP)

    def whole(relation):
        return blocks.at[block_of(relation, core)]

    def half_of(relation, rows):
        return blocks.at[block_of(relation, core), rows]

    ag_out = (
        send(whole(0), whole(0), ag, 0, z_up),
        send(whole(0), whole(0), ag, 1, z_down),
        send(whole(0), whole(0), ag, 2, x_over),
        send(half_of(1, low), half_of(1, low), ag, 3, z_up),
        send(half_of(2, high), half_of(2, high), ag, 4, z_down),
        send(whole(3), whole(3), ag, 5, z_up),
        send(whole(3), whole(3), ag, 6, z_down),
        send(whole(4), whole(4), ag, 7, x_over),
    )
    ag_in = (
        send(whole(1), whole(1), ag, 0, z_up),
        send(whole(2), whole(2), ag, 1, z_down),
        send(whole(3), whole(3), ag, 2, x_over),
        send(half_of(4, low), half_of(4, low), ag, 3, z_up),
        send(half_of(4, high), half_of(4, high), ag, 4, z_down),
        send(whole(5), whole(5), ag, 5, z_up),
        send(whole(6), whole(6), ag, 6, z_down),
        send(whole(7), whole(7), ag, 7, x_over),
    )
    sib_out = [send(whole(k), whole(k), sib, k, sibling) for k in range(8)]
    sib_in = []
    for k in range(8):
        arriving = blocks.at[block_of(k, other)]
        sib_in.append(send(arriving, arriving, sib, k, sibling))

    for number in (0, 1, 2):
        ag_out[number].start()
    sib_out[0].start()
    for copy in expert_loads:
        copy.wait()
    for piece in range(3):
        for stage in range(3):
            for copy in w_plan[piece][stage][0]:
                copy.wait_send()

    def part_of(block):
        return weight.at[block // 8, lax.rem(block // 4, 2), lax.rem(block, 4)]

    def part_rows(block, rows):
        return weight.at[block // 8, lax.rem(block // 4, 2), lax.rem(block, 4), rows]

    part = (part_send, part_recv)
    rs = (rs_send, rs_recv)
    left, right = pl.ds(0, 256), pl.ds(256, 256)
    both = pl.ds(0, 512)

    def part_copy(chip):
        return send(part_of(chip * 2 + other), sib_parts.at[chip], part, chip, sibling)

    def add_into(block, rows, extra):
        target = part_rows(block, rows)
        target[...] = (target[...].astype(jnp.float32) + extra[...].astype(jnp.float32)).astype(
            jnp.bfloat16
        )

    def chip_sum(relation):
        chip = block_of(relation, 0) // 2
        part_copy(chip).wait_recv()
        add_into(chip * 2 + core, both, sib_parts.at[chip])

    def toward(relation, rows):
        return part_rows(block_of(relation, core), rows)

    rs_out = (
        send(toward(7, left), hop_in.at[left], rs, 0, x_over),
        send(toward(7, right), hop_in.at[right], rs, 1, x_over),
        send(toward(5, both), full_in.at[2], rs, 2, z_down),
        send(toward(6, both), full_in.at[3], rs, 3, z_up),
        send(toward(1, right), full_in.at[0, right], rs, 4, z_down),
        send(toward(2, left), full_in.at[1, left], rs, 5, z_up),
        send(toward(4, left), half_in.at[0], rs, 6, z_down),
        send(toward(4, right), half_in.at[1], rs, 7, z_up),
        send(toward(3, both), far_in, rs, 8, x_over),
        send(toward(1, left), full_in.at[0, left], rs, 9, z_down),
        send(toward(2, right), full_in.at[1, right], rs, 10, z_up),
    )

    def step(number, carry):
        @pl.when(number == 0)
        def _():
            ag_in[0].wait_recv()
            ag_out[3].start()
            sib_out[1].start()
            ag_in[1].wait_recv()
            ag_out[4].start()
            sib_out[2].start()
            ag_in[2].wait_recv()
            ag_out[5].start()
            ag_out[6].start()
            sib_out[3].start()
            sib_in[0].wait_recv()
            sib_in[3].wait_recv()

        @pl.when(number == 1)
        def _():
            ag_in[3].wait_recv()
            ag_in[4].wait_recv()
            ag_out[7].start()
            sib_out[4].start()
            sib_in[1].wait_recv()
            sib_in[2].wait_recv()

        @pl.when(number == 2)
        def _():
            chip_sum(1)
            rs_out[4].start()
            chip_sum(2)
            rs_out[5].start()
            ag_in[5].wait_recv()
            sib_out[5].start()
            ag_in[6].wait_recv()
            sib_out[6].start()
            ag_in[7].wait_recv()
            sib_out[7].start()
            sib_in[4].wait_recv()
            sib_in[7].wait_recv()

        @pl.when(number == 3)
        def _():
            sib_in[5].wait_recv()
            sib_in[6].wait_recv()

        def chip_at(which):
            dz, dx = 0, 0
            for k, pair in enumerate(PAIRS):
                there = RELATIONS[pair[which]]
                dz = jnp.where(number == k, there[0], dz)
                dx = jnp.where(number == k, there[1], dx)
            return lax.rem(z + dz, 4) * 2 + lax.rem(x_high + dx, 2)

        chips = (chip_at(0), chip_at(1))
        sources = [chips[q // 2] * 2 + q % 2 for q in range(4)]
        for q in range(4):
            found = jnp.dot(
                pick[sources[q]], blocks[sources[q]], preferred_element_type=jnp.float32
            ).astype(jnp.bfloat16)
            for j in range(2):
                slots_in[j, q * CAP : (q + 1) * CAP] = found[j * CAP : (j + 1) * CAP]

        @pl.when(number == 3)
        def _():
            chip_sum(7)
            rs_out[0].start()
            rs_out[1].start()

        def expert(j, carry):
            for n in range(3):
                cols = slice(n * 256, (n + 1) * 256)
                gate_part = jnp.dot(
                    slots_in[j], gate_w[j, :, cols], preferred_element_type=jnp.float32
                )
                up_part = jnp.dot(
                    slots_in[j], up_w[j, :, cols], preferred_element_type=jnp.float32
                )
                act[:, cols] = (gate_part / (1.0 + jnp.exp(-gate_part)) * up_part).astype(
                    jnp.bfloat16
                )
            for n in range(4):
                cols = slice(n * 512, (n + 1) * 512)
                result = jnp.dot(act[...], down_w[j, :, cols], preferred_element_type=jnp.float32)
                for q in range(4):
                    slots_out[q, pl.ds(pl.multiple_of(j * CAP, CAP), CAP), cols] = result[
                        q * CAP : (q + 1) * CAP
                    ].astype(jnp.bfloat16)
            return carry

        lax.fori_loop(0, 2, expert, 0)
        for q in range(4):
            target = part_of(sources[q])
            for n in range(4):
                target[n * TOK : (n + 1) * TOK] = jnp.dot(
                    scatter[sources[q]],
                    slots_out[q, :, n * 512 : (n + 1) * 512],
                    preferred_element_type=jnp.float32,
                ).astype(jnp.bfloat16)
            if q % 2:
                part_copy(chips[q // 2]).start()
        return carry

    lax.fori_loop(0, 4, step, 0)

    chip_sum(5)
    rs_out[2].start()
    chip_sum(6)
    rs_out[3].start()
    chip_sum(4)
    rs_out[0].wait_recv()
    add_into(block_of(4, core), left, hop_in.at[left])
    rs_out[6].start()
    rs_out[1].wait_recv()
    add_into(block_of(4, core), right, hop_in.at[right])
    rs_out[7].start()
    chip_sum(3)
    chip_sum(0)
    rs_out[2].wait_recv()
    add_into(block_of(3, core), both, full_in.at[2])
    rs_out[3].wait_recv()
    add_into(block_of(3, core), both, full_in.at[3])
    rs_out[8].start()
    rs_out[6].wait_recv()
    add_into(block_of(1, core), left, half_in.at[0])
    rs_out[9].start()
    rs_out[7].wait_recv()
    add_into(block_of(2, core), right, half_in.at[1])
    rs_out[10].start()

    for number in (4, 5, 9, 10, 8):
        rs_out[number].wait_recv()
    for n in range(4):
        rows = slice(n * TOK, (n + 1) * TOK)
        cols = slice(n * 512, (n + 1) * 512)
        total = attn_resid_ref[:, cols].astype(jnp.float32)
        for extra in (part_of(exp), full_in.at[0], full_in.at[1], far_in):
            total = total + extra[rows].astype(jnp.float32)
        out_ref[:, cols] = total.astype(jnp.bfloat16)

    for copy in (*kv_out, *share_out, swap, *ag_out, *sib_out, *rs_out):
        copy.wait_send()
    for number in range(8):
        att_copy(number).wait_send()
        part_copy(number).wait_send()


def layer(*arrays):
    vmem = pl.BlockSpec(memory_space=pltpu.VMEM)
    hbm = pl.BlockSpec(memory_space=pl.ANY)
    dma = pltpu.SemaphoreType.DMA
    bf16, f32 = jnp.bfloat16, jnp.float32
    counts = (7, 32, 3, 8, 8, 36, 36, 16, 16, 8, 8, 1, 1, 8, 8, 8, 8, 8, 8, 11, 11)
    return pl.pallas_call(
        layer_kernel,
        out_shape=(
            jax.ShapeDtypeStruct((TOK, D), bf16),
            jax.ShapeDtypeStruct((TOK, D), bf16),
        ),
        in_specs=[hbm] * 11,
        out_specs=(vmem, vmem),
        scratch_shapes=[
            pltpu.VMEM((2, 2, 4, 512, 512), bf16),
            pltpu.VMEM((8, 2, TOK, 512), bf16),
            pltpu.VMEM((8, 512, HEAD_SIZE), bf16),
            pltpu.VMEM((2, TOK, 4096), bf16),
            pltpu.VMEM((2, TOK, 512), f32),
            pltpu.VMEM((4, TOK, 512), f32),
            pltpu.VMEM((TOK, D), bf16),
            pltpu.VMEM((1, D), f32),
            pltpu.VMEM((TOPK, TOK), jnp.int32),
            pltpu.VMEM((TOPK, TOK), f32),
            pltpu.VMEM((4, 8, TOK), f32),
            pltpu.VMEM((16, 8, TOK), f32),
            pltpu.VMEM((2, D, FF), bf16),
            pltpu.VMEM((2, D, FF), bf16),
            pltpu.VMEM((2, FF, D), bf16),
            pltpu.VMEM((16, TOK, D), bf16),
            pltpu.VMEM((8, 512, 512), bf16),
            pltpu.VMEM((2, 256, 512), bf16),
            pltpu.VMEM((4, 512, 512), bf16),
            pltpu.VMEM((512, 512), bf16),
            pltpu.VMEM((512, 512), bf16),
            pltpu.VMEM((2, 256, D), bf16),
            pltpu.VMEM((4, TOK, D), bf16),
            pltpu.VMEM((256, FF), bf16),
            pltpu.VMEM((16, TOK, TOK), bf16),
            pltpu.VMEM((16, TOK, TOK), bf16),
            *(dma((count,)) for count in counts),
        ],
        compiler_params=pltpu.CompilerParams(
            collective_id=0, has_side_effects=True, vmem_limit_bytes=62 << 20
        ),
    )(*arrays)


def local(
    queries,
    keys,
    values,
    resid,
    out_weight,
    norm_gain,
    expert_gate,
    expert_up,
    expert_down,
    route_ids,
    route_gates,
):
    attn_resid, layer_out = layer(
        queries[0],
        keys[0],
        values[0],
        resid[0],
        out_weight,
        norm_gain[None],
        route_ids[0].T,
        route_gates[0].T,
        expert_gate,
        expert_up,
        expert_down,
    )
    return (attn_resid[None], layer_out[None])


def solution(mesh):
    in_specs = (
        P("exp", "ctx", None),
        P("exp", "ctx", None),
        P("exp", "ctx", None),
        P("exp", "ctx", None),
        P("ctx", "exp"),
        P(),
        P("exp", None, None),
        P("exp", None, None),
        P("exp", None, None),
        P("exp", "ctx", None),
        P("exp", "ctx", None),
    )
    out_specs = (P("exp", "ctx", None), P("exp", "ctx", None))
    return jax.shard_map(local, mesh=mesh, in_specs=in_specs, out_specs=out_specs, check_vma=False)
```

```python
import functools

import jax
import jax.numpy as jnp
from jax import lax
from jax.experimental import pallas as pl
from jax.experimental.pallas import tpu as pltpu
from jax.sharding import PartitionSpec as P

QUERY_HEAD_COUNT = 32
HEAD_SIZE = 128
TOPK = 8
CAP = 64
TOK = 128
D = 2048
FF = 768
EXPERTS = 32
MESH = pl.DeviceIdType.MESH

norm_eps = 1e-06
mask_fill_value = -1e30

RELATIONS = ((0, 0), (3, 0), (1, 0), (0, 1), (2, 0), (3, 1), (1, 1), (2, 1))
ORDER = (0, 1, 2, 3, 4, 7, 5, 6)
PIECES = ((0, 208, 112, "xyz"), (208, 160, 80, "yzx"), (368, 144, 80, "zxy"))


def layer_kernel(
    queries_hbm,
    keys_hbm,
    values_hbm,
    resid_hbm,
    weight_hbm,
    gain_hbm,
    ids_hbm,
    gates_hbm,
    gate_hbm,
    up_hbm,
    down_hbm,
    attn_resid_ref,
    out_ref,
    weight,
    kv,
    stacked,
    attended,
    to_sibling,
    from_sibling,
    resid,
    gain,
    ids,
    gates,
    share_tiles,
    shares_in,
    gate_w,
    up_w,
    down_w,
    blocks,
    sib_parts,
    half_in,
    full_in,
    far_in,
    hop_in,
    slots_in,
    slots_out,
    act,
    pick,
    scatter,
    load_sem,
    query_sem,
    expert_sem,
    kv_send,
    kv_recv,
    w_send,
    w_recv,
    share_send,
    share_recv,
    att_send,
    att_recv,
    proj_send,
    proj_recv,
    ag_send,
    ag_recv,
    sib_send,
    sib_recv,
    part_send,
    part_recv,
    rs_send,
    rs_recv,
):
    ctx, exp = lax.axis_index("ctx"), lax.axis_index("exp")
    x_low, y = ctx // 4, lax.rem(ctx, 4)
    z, x_high, core = exp // 4, lax.rem(exp // 2, 2), lax.rem(exp, 2)
    here = {"x": x_high * 2 + x_low, "y": y, "z": z}
    other = 1 - core

    def device(x, y_at, z_at):
        return {"ctx": lax.rem(x, 2) * 4 + y_at, "exp": z_at * 4 + (x // 2) * 2 + core}

    def neighbour(axis, by):
        there = dict(here)
        there[axis] = lax.rem(here[axis] + by, 4)
        return device(there["x"], there["y"], there["z"])

    sibling = {"ctx": ctx, "exp": exp + 1 - 2 * core}
    partner = {"ctx": (1 - x_low) * 4 + y, "exp": exp}
    y_up, y_down = neighbour("y", 1), neighbour("y", 3)
    z_up, z_down, x_over = neighbour("z", 1), neighbour("z", 3), neighbour("x", 2)

    def send(src, dst, sems, number, peer):
        return pltpu.make_async_remote_copy(
            src_ref=src,
            dst_ref=dst,
            send_sem=sems[0].at[number],
            recv_sem=sems[1].at[number],
            device_id=peer,
            device_id_type=MESH,
        )

    own_weight = weight.at[
        x_high, x_low, y, :, pl.ds(pl.multiple_of(z * 128, 128), 128)
    ]
    loads = []
    for number, (src, dst) in enumerate(
        (
            (weight_hbm, own_weight),
            (keys_hbm, kv.at[ctx, 0]),
            (values_hbm, kv.at[ctx, 1]),
            (ids_hbm, ids),
            (gates_hbm, gates),
            (gain_hbm, gain),
            (resid_hbm, resid),
        )
    ):
        loads.append(pltpu.make_async_copy(src, dst, load_sem.at[number]))
        loads[-1].start()
    query_loads = []
    for head in range(QUERY_HEAD_COUNT):
        query_loads.append(
            pltpu.make_async_copy(
                queries_hbm.at[:, pl.ds(head * HEAD_SIZE, HEAD_SIZE)],
                stacked.at[head // 4, pl.ds((head % 4) * TOK, TOK)],
                query_sem.at[head],
            )
        )
        query_loads[-1].start()

    barrier = pltpu.get_barrier_semaphore()
    for step in range(1, 16):
        pl.semaphore_signal(
            barrier,
            inc=1,
            device_id={"ctx": ctx, "exp": lax.rem(exp + step, 16)},
            device_id_type=MESH,
        )
    for by in (1, 2, 3):
        pl.semaphore_signal(barrier, inc=1, device_id=neighbour("y", by), device_id_type=MESH)
    for by in (1, 3):
        pl.semaphore_signal(barrier, inc=1, device_id=neighbour("x", by), device_id_type=MESH)
    pl.semaphore_wait(barrier, 20)

    w_sems = (w_send, w_recv)

    def segment(piece, stage, by, rows):
        order = PIECES[piece][3]
        at = {}
        for axis in order[stage:]:
            at[axis] = here[axis]
        at[order[stage]] = lax.rem(here[order[stage]] + by, 4)
        full = slice(None)
        lanes = pl.ds(pl.multiple_of(at["z"] * 128, 128), 128) if "z" in at else full
        x_pair = (at["x"] // 2, lax.rem(at["x"], 2)) if "x" in at else (full, full)
        return weight.at[x_pair[0], x_pair[1], at.get("y", full), rows, lanes]

    def w_copies(piece, stage):
        first, height, cut, order = PIECES[piece]
        axis = order[stage]
        whole = pl.ds(first, height)
        top, bottom = pl.ds(first, cut), pl.ds(first + cut, height - cut)
        if stage < 2:
            base = piece * 12 + stage * 3
            moves = [(0, 4 - by, whole, neighbour(axis, by)) for by in (1, 3, 2)]
        else:
            base = piece * 12 + 6
            up, down = neighbour(axis, 1), neighbour(axis, 3)
            moves = [
                (0, 3, top, up),
                (0, 1, bottom, down),
                (0, 3, bottom, up),
                (0, 1, top, down),
                (3, 2, top, up),
                (1, 2, bottom, down),
            ]
        out, arrive = [], []
        for number, (sent, got, rows, peer) in enumerate(moves):
            mine = segment(piece, stage, sent, rows)
            theirs = segment(piece, stage, got, rows)
            out.append(send(mine, mine, w_sems, base + number, peer))
            arrive.append(send(theirs, theirs, w_sems, base + number, peer))
        return out, arrive

    w_plan = [[w_copies(piece, stage) for stage in range(3)] for piece in range(3)]

    def w_begin(stage):
        for number in range(3 if stage < 2 else 4):
            for piece in range(3):
                w_plan[piece][stage][0][number].start()

    def w_end(stage):
        for piece in range(3):
            for number in (0, 1, 2) if stage < 2 else (2, 3, 4, 5):
                w_plan[piece][stage][1][number].wait_recv()

    def w_forward(piece):
        out, arrive = w_plan[piece][2]
        arrive[0].wait_recv()
        out[4].start()
        arrive[1].wait_recv()
        out[5].start()

    kv_sems = (kv_send, kv_recv)

    def kv_block(dy, dx):
        return lax.rem(x_low + dx, 2) * 4 + lax.rem(y + dy, 4)

    def kv_copy(number, block, part, peer):
        ref = kv.at[block] if part is None else kv.at[block, part]
        return send(ref, ref, kv_sems, number, peer)

    kv_out = (
        kv_copy(0, kv_block(0, 0), None, y_up),
        kv_copy(1, kv_block(0, 0), None, y_down),
        kv_copy(2, kv_block(0, 0), None, partner),
        kv_copy(3, kv_block(3, 0), 0, y_up),
        kv_copy(4, kv_block(1, 0), 1, y_down),
        kv_copy(5, kv_block(0, 1), None, y_up),
        kv_copy(6, kv_block(0, 1), None, y_down),
        kv_copy(7, kv_block(2, 0), None, partner),
    )
    kv_in = (
        kv_copy(0, kv_block(3, 0), None, y_up),
        kv_copy(1, kv_block(1, 0), None, y_down),
        kv_copy(2, kv_block(0, 1), None, partner),
        kv_copy(3, kv_block(2, 0), 0, y_up),
        kv_copy(4, kv_block(2, 0), 1, y_down),
        kv_copy(5, kv_block(3, 1), None, y_up),
        kv_copy(6, kv_block(1, 1), None, y_down),
        kv_copy(7, kv_block(2, 1), None, partner),
    )

    loads[0].wait()
    w_begin(0)
    loads[1].wait()
    loads[2].wait()
    for number in (0, 1, 2):
        kv_out[number].start()
    expert_loads = []
    for number, (src, dst) in enumerate(((gate_hbm, gate_w), (up_hbm, up_w), (down_hbm, down_w))):
        expert_loads.append(pltpu.make_async_copy(src, dst, expert_sem.at[number]))
        expert_loads[-1].start()

    loads[3].wait()
    loads[4].wait()
    shares = gates[...] / jnp.sum(gates[...], axis=0, keepdims=True)
    ids_here = ids[...]
    expert_row = lax.broadcasted_iota(jnp.int32, (EXPERTS, TOK), 0)
    dense = jnp.zeros((EXPERTS, TOK), jnp.float32)
    for k in range(TOPK):
        dense = dense + jnp.where(ids_here[k : k + 1] == expert_row, shares[k : k + 1], 0.0)
    for group in range(4):
        share_tiles[group] = dense[group * 8 : (group + 1) * 8]
    shares_in[exp] = share_tiles[exp // 4]
    share_sems = (share_send, share_recv)
    share_out, share_arrive = [], []
    for step in range(1, 16):
        there = lax.rem(exp + step, 16)
        behind = lax.rem(exp + 16 - step, 16)
        peer = {"ctx": ctx, "exp": there}
        tile = share_tiles.at[there // 4]
        share_out.append(send(tile, shares_in.at[exp], share_sems, step, peer))
        share_arrive.append(send(tile, shares_in.at[behind], share_sems, step, peer))

    w_end(0)
    w_begin(1)
    for copy in share_out:
        copy.start()
    for number in (0, 1, 2):
        kv_in[number].wait_recv()
    for number in (3, 4, 5, 6):
        kv_out[number].start()
    w_end(1)
    w_begin(2)
    kv_in[3].wait_recv()
    kv_in[4].wait_recv()
    kv_out[7].start()
    for arriving in share_arrive:
        arriving.wait_recv()
    lane = lax.broadcasted_iota(jnp.int32, (TOK, TOK), 1)
    row = lax.broadcasted_iota(jnp.int32, (TOK, TOK), 0)
    up_to = (row <= lane).astype(jnp.float32).astype(jnp.bfloat16)
    slot_of_row = lax.rem(row, CAP).astype(jnp.float32)
    first_row = lax.rem(exp, 4) * 2

    def selection(block, carry):
        share_rows = jnp.concatenate(
            [
                jnp.broadcast_to(shares_in[block, pl.ds(first_row + j, 1)], (CAP, TOK))
                for j in range(2)
            ],
            axis=0,
        )
        chosen = share_rows > 0.0
        count = jnp.dot(
            chosen.astype(jnp.float32).astype(jnp.bfloat16),
            up_to,
            preferred_element_type=jnp.float32,
        )
        picked = chosen & (count - 1.0 == slot_of_row)
        pick[block] = picked.astype(jnp.float32).astype(jnp.bfloat16)
        scatter[block] = jnp.where(picked, share_rows, 0.0).T.astype(jnp.bfloat16)
        return carry

    lax.fori_loop(0, 16, selection, 0)

    for piece in range(3):
        w_forward(piece)
    for number in (5, 6, 7):
        kv_in[number].wait_recv()
    for copy in query_loads:
        copy.wait()

    att_sems = (att_send, att_recv)

    def att_copy(number):
        part = attended.at[core, :, pl.ds(pl.multiple_of(number * 512, 512), 512)]
        return send(part, part, att_sems, number, sibling)

    keys_total = 8 * TOK
    scale = HEAD_SIZE**-0.5 * 1.4426950408889634

    def heads(quad, carry):
        lanes = pl.ds(pl.multiple_of((quad // 2) * HEAD_SIZE, HEAD_SIZE), HEAD_SIZE)
        keys_here = jnp.concatenate([kv[block, 0, :, lanes] for block in range(8)], axis=0)
        values_here = jnp.concatenate([kv[block, 1, :, lanes] for block in range(8)], axis=0)
        values_wide = jnp.concatenate([values_here, jnp.ones_like(values_here)], axis=1)
        for part in range(4):
            scores = lax.dot_general(
                stacked[quad, part * TOK : (part + 1) * TOK],
                keys_here,
                (((1,), (1,)), ((), ())),
                preferred_element_type=jnp.float32,
            )
            query_at = lax.broadcasted_iota(jnp.int32, (TOK, keys_total), 0) + ctx * TOK
            key_at = lax.broadcasted_iota(jnp.int32, (TOK, keys_total), 1)
            scores = jnp.where(query_at >= key_at, scores, mask_fill_value)
            top = jnp.max(scores, axis=1, keepdims=True)
            weights = jnp.exp2((scores - top) * scale).astype(jnp.bfloat16)
            result = jnp.dot(weights, values_wide, preferred_element_type=jnp.float32)
            attended[
                core,
                :,
                pl.ds(pl.multiple_of(quad * 512 + part * HEAD_SIZE, HEAD_SIZE), HEAD_SIZE),
            ] = (result[:, :HEAD_SIZE] / result[:, HEAD_SIZE:]).astype(jnp.bfloat16)
        att_copy(quad).start()
        return carry

    lax.fori_loop(0, 8, heads, 0)

    for number in range(8):
        part = attended.at[other, :, pl.ds(number * 512, 512)]
        send(part, part, att_sems, number, sibling).wait_recv()
    w_end(2)

    def project(whose):
        def run(half, carry):
            target, at = (to_sibling, half) if whose is other else (from_sibling, 2 + half)
            target[at] = jnp.dot(
                attended[whose],
                weight[half].reshape(8 * 512, 512),
                preferred_element_type=jnp.float32,
            )
            return carry

        lax.fori_loop(0, 2, run, 0)

    project(other)
    swap = send(to_sibling, from_sibling.at[pl.ds(0, 2)], (proj_send, proj_recv), 0, sibling)
    swap.start()
    project(core)
    loads[5].wait()
    loads[6].wait()

    def place(first, which):
        for half in range(2):
            for depth in range(4):
                lanes = pl.ds(
                    pl.multiple_of(depth * 512 + half * 256 + which * 128, 128), 128
                )
                attn_resid_ref[:, lanes] = (
                    resid[:, lanes].astype(jnp.float32)
                    + from_sibling[first + half, :, depth * 128 : (depth + 1) * 128]
                ).astype(jnp.bfloat16)

    place(2, core)
    swap.wait_recv()
    place(0, other)
    wide = attn_resid_ref[...].astype(jnp.float32)
    scale_row = lax.rsqrt(jnp.mean(wide * wide, axis=1, keepdims=True) + norm_eps)
    blocks[exp] = (wide * scale_row * gain[...]).astype(jnp.bfloat16)

    def block_of(relation, which):
        dz, dx = RELATIONS[relation]
        return lax.rem(z + dz, 4) * 4 + lax.rem(x_high + dx, 2) * 2 + which

    ag = (ag_send, ag_recv)
    sib = (sib_send, sib_recv)
    low, high = pl.ds(0, CAP), pl.ds(CAP, CAP)

    def whole(relation):
        return blocks.at[block_of(relation, core)]

    def half_of(relation, rows):
        return blocks.at[block_of(relation, core), rows]

    quarters = [pl.ds(n * 32, 32) for n in range(4)]
    z_moves = (
        (0, low, 1, z_up),
        (0, high, 2, z_down),
        (0, None, 3, x_over),
        (0, high, 1, z_up),
        (0, low, 2, z_down),
        (1, quarters[0], 4, z_up),
        (2, quarters[2], 4, z_down),
        (1, quarters[1], 4, z_up),
        (2, quarters[3], 4, z_down),
        (3, None, 5, z_up),
        (3, None, 6, z_down),
        (4, quarters[0], 7, x_over),
        (4, quarters[2], 7, x_over),
        (4, quarters[1], 7, x_over),
        (4, quarters[3], 7, x_over),
    )
    ag_out, ag_in = [], []
    for number, (sent, rows, got, peer) in enumerate(z_moves):
        mine = whole(sent) if rows is None else half_of(sent, rows)
        theirs = whole(got) if rows is None else half_of(got, rows)
        ag_out.append(send(mine, mine, ag, number, peer))
        ag_in.append(send(theirs, theirs, ag, number, peer))
    sib_out = [send(whole(k), whole(k), sib, k, sibling) for k in range(8)]
    sib_in = []
    for k in range(8):
        arriving = blocks.at[block_of(k, other)]
        sib_in.append(send(arriving, arriving, sib, k, sibling))

    for number in range(5):
        ag_out[number].start()
    sib_out[0].start()
    for copy in expert_loads:
        copy.wait()
    for piece in range(3):
        for stage in range(3):
            for copy in w_plan[piece][stage][0]:
                copy.wait_send()

    def part_of(block):
        return weight.at[block // 8, lax.rem(block // 4, 2), lax.rem(block, 4)]

    def part_rows(block, rows):
        return weight.at[block // 8, lax.rem(block // 4, 2), lax.rem(block, 4), rows]

    part = (part_send, part_recv)
    rs = (rs_send, rs_recv)
    left, right = pl.ds(0, 256), pl.ds(256, 256)
    both = pl.ds(0, 512)

    def part_copy(chip):
        return send(part_of(chip * 2 + other), sib_parts.at[chip], part, chip, sibling)

    def add_into(block, rows, extra):
        target = part_rows(block, rows)
        target[...] = (target[...].astype(jnp.float32) + extra[...].astype(jnp.float32)).astype(
            jnp.bfloat16
        )

    def chip_sum(relation):
        chip = block_of(relation, 0) // 2
        part_copy(chip).wait_recv()
        add_into(chip * 2 + core, both, sib_parts.at[chip])

    def toward(relation, rows):
        return part_rows(block_of(relation, core), rows)

    fourths = [pl.ds(n * TOK, TOK) for n in range(4)]
    rs_out = [send(toward(7, rows), hop_in.at[rows], rs, n, x_over) for n, rows in enumerate(fourths)]
    rs_out.append(send(toward(5, left), full_in.at[2, left], rs, 4, z_down))
    rs_out.append(send(toward(5, right), full_in.at[2, right], rs, 5, z_down))
    rs_out.append(send(toward(6, left), full_in.at[3, left], rs, 6, z_up))
    rs_out.append(send(toward(6, right), full_in.at[3, right], rs, 7, z_up))
    rs_out.append(send(toward(1, right), full_in.at[0, right], rs, 8, z_down))
    rs_out.append(send(toward(2, left), full_in.at[1, left], rs, 9, z_up))
    for n, rows in enumerate(fourths):
        into = half_in.at[n // 2, pl.ds(n % 2 * TOK, TOK)]
        rs_out.append(send(toward(4, rows), into, rs, 10 + n, (z_down, z_up)[n // 2]))
    for n, rows in enumerate(fourths):
        into = full_in.at[n // 2, rows]
        rs_out.append(send(toward(1 + n // 2, rows), into, rs, 14 + n, (z_down, z_up)[n // 2]))
    rs_out.append(send(toward(3, left), far_in.at[left], rs, 18, x_over))
    rs_out.append(send(toward(3, right), far_in.at[right], rs, 19, x_over))

    def step(number, carry):
        @pl.when(number == 0)
        def _():
            sib_in[0].wait_recv()

        @pl.when(number == 1)
        def _():
            ag_in[0].wait_recv()
            ag_out[5].start()
            ag_out[7].start()
            ag_in[1].wait_recv()
            ag_out[6].start()
            ag_out[8].start()
            ag_in[3].wait_recv()
            sib_out[1].start()
            ag_in[4].wait_recv()
            sib_out[2].start()
            ag_in[2].wait_recv()
            sib_out[3].start()
            sib_in[1].wait_recv()

        @pl.when(number == 2)
        def _():
            for k in (5, 6):
                ag_in[k].wait_recv()
                ag_out[k + 6].start()
            ag_out[9].start()
            ag_out[10].start()
            sib_in[2].wait_recv()

        @pl.when(number == 3)
        def _():
            for k in (7, 8):
                ag_in[k].wait_recv()
                ag_out[k + 6].start()
            sib_out[4].start()
            sib_in[3].wait_recv()

        @pl.when(number == 4)
        def _():
            sib_in[4].wait_recv()

        @pl.when(number == 5)
        def _():
            chip_sum(1)
            chip_sum(2)
            ag_in[9].wait_recv()
            sib_out[5].start()
            ag_in[10].wait_recv()
            sib_out[6].start()
            rs_out[8].start()
            rs_out[9].start()
            for k in (11, 12, 13, 14):
                ag_in[k].wait_recv()
            sib_out[7].start()
            sib_in[7].wait_recv()

        @pl.when(number == 6)
        def _():
            sib_in[5].wait_recv()

        @pl.when(number == 7)
        def _():
            sib_in[6].wait_recv()

        dz, dx = 0, 0
        for k, relation in enumerate(ORDER):
            dz = jnp.where(number == k, RELATIONS[relation][0], dz)
            dx = jnp.where(number == k, RELATIONS[relation][1], dx)
        chip = lax.rem(z + dz, 4) * 2 + lax.rem(x_high + dx, 2)
        for q in range(2):
            found = jnp.dot(
                pick[chip * 2 + q], blocks[chip * 2 + q], preferred_element_type=jnp.float32
            ).astype(jnp.bfloat16)
            for j in range(2):
                slots_in[j, q * CAP : (q + 1) * CAP] = found[j * CAP : (j + 1) * CAP]

        @pl.when(number == 6)
        def _():
            chip_sum(7)
            for n in (0, 2, 1, 3):
                rs_out[n].start()
            chip_sum(4)

        @pl.when(number == 7)
        def _():
            chip_sum(5)
            rs_out[4].start()
            rs_out[5].start()

        def expert(j, carry):
            for n in range(3):
                cols = slice(n * 256, (n + 1) * 256)
                gate_part = jnp.dot(
                    slots_in[j], gate_w[j, :, cols], preferred_element_type=jnp.float32
                )
                up_part = jnp.dot(
                    slots_in[j], up_w[j, :, cols], preferred_element_type=jnp.float32
                )
                act[:, cols] = (gate_part / (1.0 + jnp.exp(-gate_part)) * up_part).astype(
                    jnp.bfloat16
                )
            for n in range(4):
                cols = slice(n * 512, (n + 1) * 512)
                result = jnp.dot(act[...], down_w[j, :, cols], preferred_element_type=jnp.float32)
                for q in range(2):
                    slots_out[q, pl.ds(pl.multiple_of(j * CAP, CAP), CAP), cols] = result[
                        q * CAP : (q + 1) * CAP
                    ].astype(jnp.bfloat16)
            return carry

        lax.fori_loop(0, 2, expert, 0)
        for which in (other, core):
            target = part_of(chip * 2 + which)
            for n in range(4):
                target[n * TOK : (n + 1) * TOK] = jnp.dot(
                    scatter[chip * 2 + which],
                    slots_out[which, :, n * 512 : (n + 1) * 512],
                    preferred_element_type=jnp.float32,
                ).astype(jnp.bfloat16)
            if which is other:
                part_copy(chip).start()
        return carry

    lax.fori_loop(0, 8, step, 0)

    chip_sum(6)
    rs_out[6].start()
    rs_out[7].start()

    def opposite(n):
        rs_out[n].wait_recv()
        add_into(block_of(4, core), fourths[n], hop_in.at[fourths[n]])
        rs_out[10 + n].start()

    def beside(n):
        rs_out[10 + n].wait_recv()
        into = half_in.at[n // 2, pl.ds(n % 2 * TOK, TOK)]
        add_into(block_of(1 + n // 2, core), fourths[n], into)
        rs_out[14 + n].start()

    def across(n, rows):
        rs_out[4 + n].wait_recv()
        add_into(block_of(3, core), rows, full_in.at[2, rows])
        rs_out[6 + n].wait_recv()
        add_into(block_of(3, core), rows, full_in.at[3, rows])
        rs_out[18 + n].start()

    opposite(0)
    opposite(2)
    chip_sum(3)
    opposite(1)
    chip_sum(0)
    opposite(3)
    beside(0)
    beside(2)
    across(0, left)
    beside(1)
    beside(3)
    across(1, right)

    rs_out[8].wait_recv()
    rs_out[9].wait_recv()
    for n in range(4):
        rows = slice(n * TOK, (n + 1) * TOK)
        cols = slice(n * 512, (n + 1) * 512)
        rs_out[14 + n].wait_recv()
        if n % 2 == 0:
            rs_out[18 + n // 2].wait_recv()
        total = attn_resid_ref[:, cols].astype(jnp.float32)
        for extra in (part_of(exp), full_in.at[0], full_in.at[1], far_in):
            total = total + extra[rows].astype(jnp.float32)
        out_ref[:, cols] = total.astype(jnp.bfloat16)

    for copy in (*kv_out, *share_out, swap, *ag_out, *sib_out, *rs_out):
        copy.wait_send()
    for number in range(8):
        att_copy(number).wait_send()
        part_copy(number).wait_send()


def layer(*arrays):
    vmem = pl.BlockSpec(memory_space=pltpu.VMEM)
    hbm = pl.BlockSpec(memory_space=pl.ANY)
    dma = pltpu.SemaphoreType.DMA
    bf16, f32 = jnp.bfloat16, jnp.float32
    counts = (7, 32, 3, 8, 8, 36, 36, 16, 16, 8, 8, 1, 1, 15, 15, 8, 8, 8, 8, 20, 20)
    return pl.pallas_call(
        layer_kernel,
        out_shape=(
            jax.ShapeDtypeStruct((TOK, D), bf16),
            jax.ShapeDtypeStruct((TOK, D), bf16),
        ),
        in_specs=[hbm] * 11,
        out_specs=(vmem, vmem),
        scratch_shapes=[
            pltpu.VMEM((2, 2, 4, 512, 512), bf16),
            pltpu.VMEM((8, 2, TOK, 512), bf16),
            pltpu.VMEM((8, 512, HEAD_SIZE), bf16),
            pltpu.VMEM((2, TOK, 4096), bf16),
            pltpu.VMEM((2, TOK, 512), f32),
            pltpu.VMEM((4, TOK, 512), f32),
            pltpu.VMEM((TOK, D), bf16),
            pltpu.VMEM((1, D), f32),
            pltpu.VMEM((TOPK, TOK), jnp.int32),
            pltpu.VMEM((TOPK, TOK), f32),
            pltpu.VMEM((4, 8, TOK), f32),
            pltpu.VMEM((16, 8, TOK), f32),
            pltpu.VMEM((2, D, FF), bf16),
            pltpu.VMEM((2, D, FF), bf16),
            pltpu.VMEM((2, FF, D), bf16),
            pltpu.VMEM((16, TOK, D), bf16),
            pltpu.VMEM((8, 512, 512), bf16),
            pltpu.VMEM((2, 256, 512), bf16),
            pltpu.VMEM((4, 512, 512), bf16),
            pltpu.VMEM((512, 512), bf16),
            pltpu.VMEM((512, 512), bf16),
            pltpu.VMEM((2, TOK, D), bf16),
            pltpu.VMEM((2, TOK, D), bf16),
            pltpu.VMEM((TOK, FF), bf16),
            pltpu.VMEM((16, TOK, TOK), bf16),
            pltpu.VMEM((16, TOK, TOK), bf16),
            *(dma((count,)) for count in counts),
        ],
        compiler_params=pltpu.CompilerParams(
            collective_id=0, has_side_effects=True, vmem_limit_bytes=62 << 20
        ),
    )(*arrays)


def local(
    queries,
    keys,
    values,
    resid,
    out_weight,
    norm_gain,
    expert_gate,
    expert_up,
    expert_down,
    route_ids,
    route_gates,
):
    attn_resid, layer_out = layer(
        queries[0],
        keys[0],
        values[0],
        resid[0],
        out_weight,
        norm_gain[None],
        route_ids[0].T,
        route_gates[0].T,
        expert_gate,
        expert_up,
        expert_down,
    )
    return (attn_resid[None], layer_out[None])


def solution(mesh):
    in_specs = (
        P("exp", "ctx", None),
        P("exp", "ctx", None),
        P("exp", "ctx", None),
        P("exp", "ctx", None),
        P("ctx", "exp"),
        P(),
        P("exp", None, None),
        P("exp", None, None),
        P("exp", None, None),
        P("exp", "ctx", None),
        P("exp", "ctx", None),
    )
    out_specs = (P("exp", "ctx", None), P("exp", "ctx", None))
    return jax.shard_map(local, mesh=mesh, in_specs=in_specs, out_specs=out_specs, check_vma=False)
```

```python
import functools

import jax
import jax.numpy as jnp
from jax import lax
from jax.experimental import pallas as pl
from jax.experimental.pallas import tpu as pltpu
from jax.sharding import PartitionSpec as P

QUERY_HEAD_COUNT = 32
HEAD_SIZE = 128
TOPK = 8
CAP = 64
TOK = 128
D = 2048
FF = 768
EXPERTS = 32
MESH = pl.DeviceIdType.MESH

norm_eps = 1e-06
mask_fill_value = -1e30

RELATIONS = ((0, 0), (3, 0), (1, 0), (0, 1), (2, 0), (3, 1), (1, 1), (2, 1))
ORDER = (0, 1, 2, 3, 4, 7, 5, 6)
PIECES = ((0, 208, 112, "xyz"), (208, 160, 80, "yzx"), (368, 144, 80, "zxy"))


def layer_kernel(
    queries_hbm,
    keys_hbm,
    values_hbm,
    resid_hbm,
    weight_hbm,
    gain_hbm,
    ids_hbm,
    gates_hbm,
    gate_hbm,
    up_hbm,
    down_hbm,
    outs_ref,
    weight,
    kv,
    stacked,
    attended,
    to_sibling,
    from_sibling,
    resid,
    gain,
    ids,
    gates,
    share_tiles,
    shares_in,
    gate_w,
    up_w,
    down_w,
    blocks,
    sib_parts,
    half_in,
    full_in,
    far_in,
    hop_in,
    slots_in,
    slots_out,
    act,
    pick,
    scatter,
    load_sem,
    query_sem,
    expert_sem,
    kv_send,
    kv_recv,
    w_send,
    w_recv,
    share_send,
    share_recv,
    att_send,
    att_recv,
    proj_send,
    proj_recv,
    ag_send,
    ag_recv,
    sib_send,
    sib_recv,
    part_send,
    part_recv,
    rs_send,
    rs_recv,
):
    attn_resid_ref, out_ref = outs_ref.at[0], outs_ref.at[1]
    ctx, exp = lax.axis_index("ctx"), lax.axis_index("exp")
    x_low, y = ctx // 4, lax.rem(ctx, 4)
    z, x_high, core = exp // 4, lax.rem(exp // 2, 2), lax.rem(exp, 2)
    here = {"x": x_high * 2 + x_low, "y": y, "z": z}
    other = 1 - core

    def device(x, y_at, z_at):
        return {"ctx": lax.rem(x, 2) * 4 + y_at, "exp": z_at * 4 + (x // 2) * 2 + core}

    def neighbour(axis, by):
        there = dict(here)
        there[axis] = lax.rem(here[axis] + by, 4)
        return device(there["x"], there["y"], there["z"])

    sibling = {"ctx": ctx, "exp": exp + 1 - 2 * core}
    partner = {"ctx": (1 - x_low) * 4 + y, "exp": exp}
    y_up, y_down = neighbour("y", 1), neighbour("y", 3)
    z_up, z_down, x_over = neighbour("z", 1), neighbour("z", 3), neighbour("x", 2)

    def send(src, dst, sems, number, peer):
        return pltpu.make_async_remote_copy(
            src_ref=src,
            dst_ref=dst,
            send_sem=sems[0].at[number],
            recv_sem=sems[1].at[number],
            device_id=peer,
            device_id_type=MESH,
        )

    own_weight = weight.at[
        x_high, x_low, y, :, pl.ds(pl.multiple_of(z * 128, 128), 128)
    ]
    loads = []
    for number, (src, dst) in enumerate(
        (
            (weight_hbm, own_weight),
            (keys_hbm, kv.at[ctx, 0]),
            (values_hbm, kv.at[ctx, 1]),
            (ids_hbm, ids),
            (gates_hbm, gates),
            (gain_hbm, gain),
            (resid_hbm, resid),
        )
    ):
        loads.append(pltpu.make_async_copy(src, dst, load_sem.at[number]))
        loads[-1].start()
    query_loads = []
    for head in range(QUERY_HEAD_COUNT):
        query_loads.append(
            pltpu.make_async_copy(
                queries_hbm.at[:, pl.ds(head * HEAD_SIZE, HEAD_SIZE)],
                stacked.at[head // 4, pl.ds((head % 4) * TOK, TOK)],
                query_sem.at[head],
            )
        )
        query_loads[-1].start()

    barrier = pltpu.get_barrier_semaphore()
    for step in range(1, 16):
        pl.semaphore_signal(
            barrier,
            inc=1,
            device_id={"ctx": ctx, "exp": lax.rem(exp + step, 16)},
            device_id_type=MESH,
        )
    for by in (1, 2, 3):
        pl.semaphore_signal(barrier, inc=1, device_id=neighbour("y", by), device_id_type=MESH)
    for by in (1, 3):
        pl.semaphore_signal(barrier, inc=1, device_id=neighbour("x", by), device_id_type=MESH)
    pl.semaphore_wait(barrier, 20)

    w_sems = (w_send, w_recv)

    def segment(piece, stage, by, rows):
        order = PIECES[piece][3]
        at = {}
        for axis in order[stage:]:
            at[axis] = here[axis]
        at[order[stage]] = lax.rem(here[order[stage]] + by, 4)
        full = slice(None)
        lanes = pl.ds(pl.multiple_of(at["z"] * 128, 128), 128) if "z" in at else full
        x_pair = (at["x"] // 2, lax.rem(at["x"], 2)) if "x" in at else (full, full)
        return weight.at[x_pair[0], x_pair[1], at.get("y", full), rows, lanes]

    def w_copies(piece, stage):
        first, height, cut, order = PIECES[piece]
        axis = order[stage]
        whole = pl.ds(first, height)
        top, bottom = pl.ds(first, cut), pl.ds(first + cut, height - cut)
        if stage < 2:
            base = piece * 12 + stage * 3
            moves = [(0, 4 - by, whole, neighbour(axis, by)) for by in (1, 3, 2)]
        else:
            base = piece * 12 + 6
            up, down = neighbour(axis, 1), neighbour(axis, 3)
            moves = [
                (0, 3, top, up),
                (0, 1, bottom, down),
                (0, 3, bottom, up),
                (0, 1, top, down),
                (3, 2, top, up),
                (1, 2, bottom, down),
            ]
        out, arrive = [], []
        for number, (sent, got, rows, peer) in enumerate(moves):
            mine = segment(piece, stage, sent, rows)
            theirs = segment(piece, stage, got, rows)
            out.append(send(mine, mine, w_sems, base + number, peer))
            arrive.append(send(theirs, theirs, w_sems, base + number, peer))
        return out, arrive

    w_plan = [[w_copies(piece, stage) for stage in range(3)] for piece in range(3)]

    def w_begin(stage):
        for number in range(3 if stage < 2 else 4):
            for piece in range(3):
                w_plan[piece][stage][0][number].start()

    def w_end(stage):
        for piece in range(3):
            for number in (0, 1, 2) if stage < 2 else (2, 3, 4, 5):
                w_plan[piece][stage][1][number].wait_recv()

    def w_forward(piece):
        out, arrive = w_plan[piece][2]
        arrive[0].wait_recv()
        out[4].start()
        arrive[1].wait_recv()
        out[5].start()

    kv_sems = (kv_send, kv_recv)

    def kv_block(dy, dx):
        return lax.rem(x_low + dx, 2) * 4 + lax.rem(y + dy, 4)

    def kv_copy(number, block, part, peer):
        ref = kv.at[block] if part is None else kv.at[block, part]
        return send(ref, ref, kv_sems, number, peer)

    kv_out = (
        kv_copy(0, kv_block(0, 0), None, y_up),
        kv_copy(1, kv_block(0, 0), None, y_down),
        kv_copy(2, kv_block(0, 0), None, partner),
        kv_copy(3, kv_block(3, 0), 0, y_up),
        kv_copy(4, kv_block(1, 0), 1, y_down),
        kv_copy(5, kv_block(0, 1), None, y_up),
        kv_copy(6, kv_block(0, 1), None, y_down),
        kv_copy(7, kv_block(2, 0), None, partner),
    )
    kv_in = (
        kv_copy(0, kv_block(3, 0), None, y_up),
        kv_copy(1, kv_block(1, 0), None, y_down),
        kv_copy(2, kv_block(0, 1), None, partner),
        kv_copy(3, kv_block(2, 0), 0, y_up),
        kv_copy(4, kv_block(2, 0), 1, y_down),
        kv_copy(5, kv_block(3, 1), None, y_up),
        kv_copy(6, kv_block(1, 1), None, y_down),
        kv_copy(7, kv_block(2, 1), None, partner),
    )

    loads[0].wait()
    w_begin(0)
    loads[1].wait()
    loads[2].wait()
    for number in (0, 1, 2):
        kv_out[number].start()
    expert_loads = []
    for number, (src, dst) in enumerate(((gate_hbm, gate_w), (up_hbm, up_w), (down_hbm, down_w))):
        expert_loads.append(pltpu.make_async_copy(src, dst, expert_sem.at[number]))
        expert_loads[-1].start()

    loads[3].wait()
    loads[4].wait()
    shares = gates[...] / jnp.sum(gates[...], axis=0, keepdims=True)
    ids_here = ids[...]
    expert_row = lax.broadcasted_iota(jnp.int32, (EXPERTS, TOK), 0)
    dense = jnp.zeros((EXPERTS, TOK), jnp.float32)
    for k in range(TOPK):
        dense = dense + jnp.where(ids_here[k : k + 1] == expert_row, shares[k : k + 1], 0.0)
    for group in range(4):
        share_tiles[group] = dense[group * 8 : (group + 1) * 8]
    shares_in[exp] = share_tiles[exp // 4]
    share_sems = (share_send, share_recv)
    share_out, share_arrive = [], []
    for step in range(1, 16):
        there = lax.rem(exp + step, 16)
        behind = lax.rem(exp + 16 - step, 16)
        peer = {"ctx": ctx, "exp": there}
        tile = share_tiles.at[there // 4]
        share_out.append(send(tile, shares_in.at[exp], share_sems, step, peer))
        share_arrive.append(send(tile, shares_in.at[behind], share_sems, step, peer))

    w_end(0)
    w_begin(1)
    for copy in share_out:
        copy.start()
    for number in (0, 1, 2):
        kv_in[number].wait_recv()
    for number in (3, 4, 5, 6):
        kv_out[number].start()
    w_end(1)
    w_begin(2)
    kv_in[3].wait_recv()
    kv_in[4].wait_recv()
    kv_out[7].start()
    for arriving in share_arrive:
        arriving.wait_recv()
    lane = lax.broadcasted_iota(jnp.int32, (TOK, TOK), 1)
    row = lax.broadcasted_iota(jnp.int32, (TOK, TOK), 0)
    up_to = (row <= lane).astype(jnp.float32).astype(jnp.bfloat16)
    slot_of_row = lax.rem(row, CAP).astype(jnp.float32)
    first_row = lax.rem(exp, 4) * 2

    def selection(block, carry):
        share_rows = jnp.concatenate(
            [
                jnp.broadcast_to(shares_in[block, pl.ds(first_row + j, 1)], (CAP, TOK))
                for j in range(2)
            ],
            axis=0,
        )
        chosen = share_rows > 0.0
        count = jnp.dot(
            chosen.astype(jnp.float32).astype(jnp.bfloat16),
            up_to,
            preferred_element_type=jnp.float32,
        )
        picked = chosen & (count - 1.0 == slot_of_row)
        pick[block] = picked.astype(jnp.float32).astype(jnp.bfloat16)
        scatter[block] = jnp.where(picked, share_rows, 0.0).T.astype(jnp.bfloat16)
        return carry

    lax.fori_loop(0, 16, selection, 0)

    for piece in range(3):
        w_forward(piece)
    for number in (5, 6, 7):
        kv_in[number].wait_recv()
    for copy in query_loads:
        copy.wait()

    att_sems = (att_send, att_recv)

    def att_copy(number):
        part = attended.at[core, :, pl.ds(pl.multiple_of(number * 512, 512), 512)]
        return send(part, part, att_sems, number, sibling)

    keys_total = 8 * TOK
    scale = HEAD_SIZE**-0.5 * 1.4426950408889634

    def heads(quad, carry):
        lanes = pl.ds(pl.multiple_of((quad // 2) * HEAD_SIZE, HEAD_SIZE), HEAD_SIZE)
        keys_here = jnp.concatenate([kv[block, 0, :, lanes] for block in range(8)], axis=0)
        values_here = jnp.concatenate([kv[block, 1, :, lanes] for block in range(8)], axis=0)
        values_wide = jnp.concatenate([values_here, jnp.ones_like(values_here)], axis=1)
        for part in range(4):
            scores = lax.dot_general(
                stacked[quad, part * TOK : (part + 1) * TOK],
                keys_here,
                (((1,), (1,)), ((), ())),
                preferred_element_type=jnp.float32,
            )
            query_at = lax.broadcasted_iota(jnp.int32, (TOK, keys_total), 0) + ctx * TOK
            key_at = lax.broadcasted_iota(jnp.int32, (TOK, keys_total), 1)
            scores = jnp.where(query_at >= key_at, scores, mask_fill_value)
            top = jnp.max(scores, axis=1, keepdims=True)
            weights = jnp.exp2((scores - top) * scale).astype(jnp.bfloat16)
            result = jnp.dot(weights, values_wide, preferred_element_type=jnp.float32)
            attended[
                core,
                :,
                pl.ds(pl.multiple_of(quad * 512 + part * HEAD_SIZE, HEAD_SIZE), HEAD_SIZE),
            ] = (result[:, :HEAD_SIZE] / result[:, HEAD_SIZE:]).astype(jnp.bfloat16)
        att_copy(quad).start()
        return carry

    lax.fori_loop(0, 8, heads, 0)

    for number in range(8):
        part = attended.at[other, :, pl.ds(number * 512, 512)]
        send(part, part, att_sems, number, sibling).wait_recv()
    w_end(2)

    def project(whose):
        def run(half, carry):
            target, at = (to_sibling, half) if whose is other else (from_sibling, 2 + half)
            target[at] = jnp.dot(
                attended[whose],
                weight[half].reshape(8 * 512, 512),
                preferred_element_type=jnp.float32,
            )
            return carry

        lax.fori_loop(0, 2, run, 0)

    project(other)
    swap = send(to_sibling, from_sibling.at[pl.ds(0, 2)], (proj_send, proj_recv), 0, sibling)
    swap.start()
    project(core)
    loads[5].wait()
    loads[6].wait()

    def place(first, which):
        for half in range(2):
            for depth in range(4):
                lanes = pl.ds(
                    pl.multiple_of(depth * 512 + half * 256 + which * 128, 128), 128
                )
                attn_resid_ref[:, lanes] = (
                    resid[:, lanes].astype(jnp.float32)
                    + from_sibling[first + half, :, depth * 128 : (depth + 1) * 128]
                ).astype(jnp.bfloat16)

    place(2, core)
    swap.wait_recv()
    place(0, other)
    wide = attn_resid_ref[...].astype(jnp.float32)
    scale_row = lax.rsqrt(jnp.mean(wide * wide, axis=1, keepdims=True) + norm_eps)
    blocks[exp] = (wide * scale_row * gain[...]).astype(jnp.bfloat16)

    def block_of(relation, which):
        dz, dx = RELATIONS[relation]
        return lax.rem(z + dz, 4) * 4 + lax.rem(x_high + dx, 2) * 2 + which

    ag = (ag_send, ag_recv)
    sib = (sib_send, sib_recv)
    low, high = pl.ds(0, CAP), pl.ds(CAP, CAP)

    def whole(relation):
        return blocks.at[block_of(relation, core)]

    def half_of(relation, rows):
        return blocks.at[block_of(relation, core), rows]

    quarters = [pl.ds(n * 32, 32) for n in range(4)]
    z_moves = (
        (0, low, 1, z_up),
        (0, high, 2, z_down),
        (0, None, 3, x_over),
        (0, high, 1, z_up),
        (0, low, 2, z_down),
        (1, quarters[0], 4, z_up),
        (2, quarters[2], 4, z_down),
        (1, quarters[1], 4, z_up),
        (2, quarters[3], 4, z_down),
        (3, None, 5, z_up),
        (3, None, 6, z_down),
        (4, quarters[0], 7, x_over),
        (4, quarters[2], 7, x_over),
        (4, quarters[1], 7, x_over),
        (4, quarters[3], 7, x_over),
    )
    ag_out, ag_in = [], []
    for number, (sent, rows, got, peer) in enumerate(z_moves):
        mine = whole(sent) if rows is None else half_of(sent, rows)
        theirs = whole(got) if rows is None else half_of(got, rows)
        ag_out.append(send(mine, mine, ag, number, peer))
        ag_in.append(send(theirs, theirs, ag, number, peer))
    sib_out = [send(whole(k), whole(k), sib, k, sibling) for k in range(8)]
    sib_in = []
    for k in range(8):
        arriving = blocks.at[block_of(k, other)]
        sib_in.append(send(arriving, arriving, sib, k, sibling))

    for number in range(5):
        ag_out[number].start()
    sib_out[0].start()
    for copy in expert_loads:
        copy.wait()
    for piece in range(3):
        for stage in range(3):
            for copy in w_plan[piece][stage][0]:
                copy.wait_send()

    def part_of(block):
        return weight.at[block // 8, lax.rem(block // 4, 2), lax.rem(block, 4)]

    def part_rows(block, rows):
        return weight.at[block // 8, lax.rem(block // 4, 2), lax.rem(block, 4), rows]

    part = (part_send, part_recv)
    rs = (rs_send, rs_recv)
    left, right = pl.ds(0, 256), pl.ds(256, 256)
    both = pl.ds(0, 512)

    def part_copy(chip):
        return send(part_of(chip * 2 + other), sib_parts.at[chip], part, chip, sibling)

    def add_into(block, rows, extra):
        target = part_rows(block, rows)
        target[...] = (target[...].astype(jnp.float32) + extra[...].astype(jnp.float32)).astype(
            jnp.bfloat16
        )

    def chip_sum(relation):
        chip = block_of(relation, 0) // 2
        part_copy(chip).wait_recv()
        add_into(chip * 2 + core, both, sib_parts.at[chip])

    def toward(relation, rows):
        return part_rows(block_of(relation, core), rows)

    fourths = [pl.ds(n * TOK, TOK) for n in range(4)]
    rs_out = []

    def rs_send_rows(relation, rows, into, peer):
        rs_out.append(send(toward(relation, rows), into, rs, len(rs_out), peer))

    def quarter_in(n):
        return half_in.at[n // 2, pl.ds(n % 2 * TOK, TOK)]

    z_way = (z_down, z_down, z_up, z_up)
    for n, rows in enumerate(fourths):
        rs_send_rows(4, rows, quarter_in(n), z_way[n])
    rs_send_rows(1, right, full_in.at[0, right], z_down)
    rs_send_rows(2, left, full_in.at[1, left], z_up)
    for n, rows in enumerate(fourths):
        rs_send_rows(1 + n // 2, rows, full_in.at[n // 2, rows], z_way[n])
    for n, rows in enumerate(fourths):
        rs_send_rows(7, rows, hop_in.at[rows], z_way[n])
    rs_send_rows(5, right, full_in.at[2, right], z_down)
    rs_send_rows(6, left, full_in.at[3, left], z_up)
    for n, rows in enumerate(fourths):
        rs_send_rows(5 + n // 2, rows, full_in.at[2 + n // 2, rows], z_way[n])
    for rows in fourths:
        rs_send_rows(3, rows, far_in.at[rows], x_over)

    def beside(n):
        rs_out[n].wait_recv()
        add_into(block_of(1 + n // 2, core), fourths[n], quarter_in(n))
        rs_out[6 + n].start()

    def beside_other(n):
        rs_out[10 + n].wait_recv()
        add_into(block_of(5 + n // 2, core), fourths[n], hop_in.at[fourths[n]])
        rs_out[16 + n].start()

    def across(n):
        rs_out[16 + n].wait_recv()
        target = toward(3, fourths[n])
        target[...] = (
            target[...].astype(jnp.float32)
            + full_in[2, fourths[n]].astype(jnp.float32)
            + full_in[3, fourths[n]].astype(jnp.float32)
        ).astype(jnp.bfloat16)
        rs_out[20 + n].start()

    def step(number, carry):
        @pl.when(number == 0)
        def _():
            sib_in[0].wait_recv()

        @pl.when(number == 1)
        def _():
            ag_in[0].wait_recv()
            ag_out[5].start()
            ag_out[7].start()
            ag_in[1].wait_recv()
            ag_out[6].start()
            ag_out[8].start()
            ag_in[3].wait_recv()
            sib_out[1].start()
            ag_in[4].wait_recv()
            sib_out[2].start()
            ag_in[2].wait_recv()
            sib_out[3].start()
            sib_in[1].wait_recv()

        @pl.when(number == 2)
        def _():
            for k in (5, 6):
                ag_in[k].wait_recv()
                ag_out[k + 6].start()
            ag_out[9].start()
            ag_out[10].start()
            sib_in[2].wait_recv()

        @pl.when(number == 3)
        def _():
            for k in (7, 8):
                ag_in[k].wait_recv()
                ag_out[k + 6].start()
            sib_out[4].start()
            sib_in[3].wait_recv()

        @pl.when(number == 4)
        def _():
            sib_in[4].wait_recv()

        @pl.when(number == 5)
        def _():
            chip_sum(1)
            chip_sum(2)
            ag_in[9].wait_recv()
            sib_out[5].start()
            ag_in[10].wait_recv()
            sib_out[6].start()
            chip_sum(4)
            for n in (0, 2, 1, 3, 4, 5):
                rs_out[n].start()
            for k in (11, 12, 13, 14):
                ag_in[k].wait_recv()
            sib_out[7].start()
            sib_in[7].wait_recv()

        @pl.when(number == 6)
        def _():
            sib_in[5].wait_recv()

        @pl.when(number == 7)
        def _():
            sib_in[6].wait_recv()

        dz, dx = 0, 0
        for k, relation in enumerate(ORDER):
            dz = jnp.where(number == k, RELATIONS[relation][0], dz)
            dx = jnp.where(number == k, RELATIONS[relation][1], dx)
        chip = lax.rem(z + dz, 4) * 2 + lax.rem(x_high + dx, 2)
        for q in range(2):
            found = jnp.dot(
                pick[chip * 2 + q], blocks[chip * 2 + q], preferred_element_type=jnp.float32
            ).astype(jnp.bfloat16)
            for j in range(2):
                slots_in[j, q * CAP : (q + 1) * CAP] = found[j * CAP : (j + 1) * CAP]

        @pl.when(number == 6)
        def _():
            chip_sum(7)
            for n in (0, 2, 1, 3):
                rs_out[10 + n].start()
            beside(0)
            beside(2)

        @pl.when(number == 7)
        def _():
            chip_sum(5)
            rs_out[14].start()
            beside(1)
            beside(3)

        def expert(j, carry):
            for n in range(3):
                cols = slice(n * 256, (n + 1) * 256)
                gate_part = jnp.dot(
                    slots_in[j], gate_w[j, :, cols], preferred_element_type=jnp.float32
                )
                up_part = jnp.dot(
                    slots_in[j], up_w[j, :, cols], preferred_element_type=jnp.float32
                )
                act[:, cols] = (gate_part / (1.0 + jnp.exp(-gate_part)) * up_part).astype(
                    jnp.bfloat16
                )
            for n in range(4):
                cols = slice(n * 512, (n + 1) * 512)
                result = jnp.dot(act[...], down_w[j, :, cols], preferred_element_type=jnp.float32)
                for q in range(2):
                    slots_out[q, pl.ds(pl.multiple_of(j * CAP, CAP), CAP), cols] = result[
                        q * CAP : (q + 1) * CAP
                    ].astype(jnp.bfloat16)
            return carry

        lax.fori_loop(0, 2, expert, 0)
        for which in (other, core):
            target = part_of(chip * 2 + which)
            for n in range(4):
                target[n * TOK : (n + 1) * TOK] = jnp.dot(
                    scatter[chip * 2 + which],
                    slots_out[which, :, n * 512 : (n + 1) * 512],
                    preferred_element_type=jnp.float32,
                ).astype(jnp.bfloat16)
            if which is other:
                part_copy(chip).start()
        return carry

    lax.fori_loop(0, 8, step, 0)

    chip_sum(6)
    rs_out[15].start()
    for n in (0, 2, 1, 3):
        beside_other(n)
    chip_sum(3)
    chip_sum(0)
    rs_out[15].wait_recv()
    across(0)
    rs_out[14].wait_recv()
    across(2)
    across(1)
    across(3)

    rs_out[4].wait_recv()
    rs_out[5].wait_recv()
    for n in (0, 2, 1, 3):
        rows = slice(n * TOK, (n + 1) * TOK)
        cols = slice(n * 512, (n + 1) * 512)
        rs_out[6 + n].wait_recv()
        rs_out[20 + n].wait_recv()
        total = attn_resid_ref[:, cols].astype(jnp.float32)
        for extra in (part_of(exp), full_in.at[0], full_in.at[1], far_in):
            total = total + extra[rows].astype(jnp.float32)
        out_ref[:, cols] = total.astype(jnp.bfloat16)

    for copy in (*kv_out, *share_out, swap, *ag_out, *sib_out, *rs_out):
        copy.wait_send()
    for number in range(8):
        att_copy(number).wait_send()
        part_copy(number).wait_send()


def layer(*arrays):
    vmem = pl.BlockSpec(memory_space=pltpu.VMEM)
    hbm = pl.BlockSpec(memory_space=pl.ANY)
    dma = pltpu.SemaphoreType.DMA
    bf16, f32 = jnp.bfloat16, jnp.float32
    counts = (7, 32, 3, 8, 8, 36, 36, 16, 16, 8, 8, 1, 1, 15, 15, 8, 8, 8, 8, 24, 24)
    return pl.pallas_call(
        layer_kernel,
        out_shape=jax.ShapeDtypeStruct((2, TOK, D), bf16),
        in_specs=[hbm] * 11,
        out_specs=vmem,
        scratch_shapes=[
            pltpu.VMEM((2, 2, 4, 512, 512), bf16),
            pltpu.VMEM((8, 2, TOK, 512), bf16),
            pltpu.VMEM((8, 512, HEAD_SIZE), bf16),
            pltpu.VMEM((2, TOK, 4096), bf16),
            pltpu.VMEM((2, TOK, 512), f32),
            pltpu.VMEM((4, TOK, 512), f32),
            pltpu.VMEM((TOK, D), bf16),
            pltpu.VMEM((1, D), f32),
            pltpu.VMEM((TOPK, TOK), jnp.int32),
            pltpu.VMEM((TOPK, TOK), f32),
            pltpu.VMEM((4, 8, TOK), f32),
            pltpu.VMEM((16, 8, TOK), f32),
            pltpu.VMEM((2, D, FF), bf16),
            pltpu.VMEM((2, D, FF), bf16),
            pltpu.VMEM((2, FF, D), bf16),
            pltpu.VMEM((16, TOK, D), bf16),
            pltpu.VMEM((8, 512, 512), bf16),
            pltpu.VMEM((2, 256, 512), bf16),
            pltpu.VMEM((4, 512, 512), bf16),
            pltpu.VMEM((512, 512), bf16),
            pltpu.VMEM((512, 512), bf16),
            pltpu.VMEM((2, TOK, D), bf16),
            pltpu.VMEM((2, TOK, D), bf16),
            pltpu.VMEM((TOK, FF), bf16),
            pltpu.VMEM((16, TOK, TOK), bf16),
            pltpu.VMEM((16, TOK, TOK), bf16),
            *(dma((count,)) for count in counts),
        ],
        compiler_params=pltpu.CompilerParams(
            collective_id=0, has_side_effects=True, vmem_limit_bytes=62 << 20
        ),
    )(*arrays)


def local(
    queries,
    keys,
    values,
    resid,
    out_weight,
    norm_gain,
    expert_gate,
    expert_up,
    expert_down,
    route_ids,
    route_gates,
):
    outs = layer(
        queries[0],
        keys[0],
        values[0],
        resid[0],
        out_weight,
        norm_gain[None],
        route_ids[0].T,
        route_gates[0].T,
        expert_gate,
        expert_up,
        expert_down,
    )
    return (outs[0][None], outs[1][None])


def solution(mesh):
    in_specs = (
        P("exp", "ctx", None),
        P("exp", "ctx", None),
        P("exp", "ctx", None),
        P("exp", "ctx", None),
        P("ctx", "exp"),
        P(),
        P("exp", None, None),
        P("exp", None, None),
        P("exp", None, None),
        P("exp", "ctx", None),
        P("exp", "ctx", None),
    )
    out_specs = (P("exp", "ctx", None), P("exp", "ctx", None))
    return jax.shard_map(local, mesh=mesh, in_specs=in_specs, out_specs=out_specs, check_vma=False)
```

```python
import functools

import jax
import jax.numpy as jnp
from jax import lax
from jax.experimental import pallas as pl
from jax.experimental.pallas import tpu as pltpu
from jax.sharding import PartitionSpec as P

QUERY_HEAD_COUNT = 32
HEAD_SIZE = 128
TOPK = 8
CAP = 64
TOK = 128
D = 2048
FF = 768
EXPERTS = 32
MESH = pl.DeviceIdType.MESH

norm_eps = 1e-06
mask_fill_value = -1e30

RELATIONS = ((0, 0), (3, 0), (1, 0), (0, 1), (2, 0), (3, 1), (1, 1), (2, 1))
ORDER = (0, 1, 2, 3, 4, 7, 5, 6)
PIECES = ((0, 192, 96, "yxz"), (192, 160, 80, "zyx"), (352, 160, 80, "xzy"))


def layer_kernel(
    queries_hbm,
    keys_hbm,
    values_hbm,
    resid_hbm,
    weight_hbm,
    gain_hbm,
    ids_hbm,
    gates_hbm,
    gate_hbm,
    up_hbm,
    down_hbm,
    outs_ref,
    weight,
    kv,
    stacked,
    attended,
    to_sibling,
    from_sibling,
    resid,
    gain,
    ids,
    gates,
    share_tiles,
    shares_in,
    gate_w,
    up_w,
    down_w,
    blocks,
    sib_parts,
    half_in,
    full_in,
    far_in,
    hop_in,
    x_in,
    slots_in,
    slots_out,
    act,
    pick,
    scatter,
    load_sem,
    query_sem,
    expert_sem,
    kv_send,
    kv_recv,
    w_send,
    w_recv,
    share_send,
    share_recv,
    att_send,
    att_recv,
    proj_send,
    proj_recv,
    ag_send,
    ag_recv,
    sib_send,
    sib_recv,
    part_send,
    part_recv,
    rs_send,
    rs_recv,
):
    attn_resid_ref, out_ref = outs_ref.at[0], outs_ref.at[1]
    ctx, exp = lax.axis_index("ctx"), lax.axis_index("exp")
    x_low, y = ctx // 4, lax.rem(ctx, 4)
    z, x_high, core = exp // 4, lax.rem(exp // 2, 2), lax.rem(exp, 2)
    here = {"x": x_high * 2 + x_low, "y": y, "z": z}
    other = 1 - core

    def device(x, y_at, z_at):
        return {"ctx": lax.rem(x, 2) * 4 + y_at, "exp": z_at * 4 + (x // 2) * 2 + core}

    def neighbour(axis, by):
        there = dict(here)
        there[axis] = lax.rem(here[axis] + by, 4)
        return device(there["x"], there["y"], there["z"])

    sibling = {"ctx": ctx, "exp": exp + 1 - 2 * core}
    partner = {"ctx": (1 - x_low) * 4 + y, "exp": exp}
    y_up, y_down = neighbour("y", 1), neighbour("y", 3)
    z_up, z_down, x_over = neighbour("z", 1), neighbour("z", 3), neighbour("x", 2)

    def send(src, dst, sems, number, peer):
        return pltpu.make_async_remote_copy(
            src_ref=src,
            dst_ref=dst,
            send_sem=sems[0].at[number],
            recv_sem=sems[1].at[number],
            device_id=peer,
            device_id_type=MESH,
        )

    own_weight = weight.at[
        x_high, x_low, y, :, pl.ds(pl.multiple_of(z * 128, 128), 128)
    ]
    loads = []
    for number, (src, dst) in enumerate(
        (
            (weight_hbm, own_weight),
            (keys_hbm, kv.at[ctx, 0]),
            (values_hbm, kv.at[ctx, 1]),
            (ids_hbm, ids),
            (gates_hbm, gates),
            (gain_hbm, gain),
            (resid_hbm, resid),
        )
    ):
        loads.append(pltpu.make_async_copy(src, dst, load_sem.at[number]))
        loads[-1].start()
    query_loads = []
    for head in range(QUERY_HEAD_COUNT):
        query_loads.append(
            pltpu.make_async_copy(
                queries_hbm.at[:, pl.ds(head * HEAD_SIZE, HEAD_SIZE)],
                stacked.at[head // 4, pl.ds((head % 4) * TOK, TOK)],
                query_sem.at[head],
            )
        )
        query_loads[-1].start()

    barrier = pltpu.get_barrier_semaphore()
    for step in range(1, 16):
        pl.semaphore_signal(
            barrier,
            inc=1,
            device_id={"ctx": ctx, "exp": lax.rem(exp + step, 16)},
            device_id_type=MESH,
        )
    for by in (1, 2, 3):
        pl.semaphore_signal(barrier, inc=1, device_id=neighbour("y", by), device_id_type=MESH)
    for by in (1, 3):
        pl.semaphore_signal(barrier, inc=1, device_id=neighbour("x", by), device_id_type=MESH)
    pl.semaphore_wait(barrier, 20)

    w_sems = (w_send, w_recv)

    def segment(piece, stage, by, rows):
        order = PIECES[piece][3]
        at = {}
        for axis in order[stage:]:
            at[axis] = here[axis]
        at[order[stage]] = lax.rem(here[order[stage]] + by, 4)
        full = slice(None)
        lanes = pl.ds(pl.multiple_of(at["z"] * 128, 128), 128) if "z" in at else full
        x_pair = (at["x"] // 2, lax.rem(at["x"], 2)) if "x" in at else (full, full)
        return weight.at[x_pair[0], x_pair[1], at.get("y", full), rows, lanes]

    def w_copies(piece, stage):
        first, height, cut, order = PIECES[piece]
        axis = order[stage]
        whole = pl.ds(first, height)
        top, bottom = pl.ds(first, cut), pl.ds(first + cut, height - cut)
        if stage < 2:
            base = piece * 12 + stage * 3
            moves = [(0, 4 - by, whole, neighbour(axis, by)) for by in (1, 3, 2)]
        else:
            base = piece * 12 + 6
            up, down = neighbour(axis, 1), neighbour(axis, 3)
            moves = [
                (0, 3, top, up),
                (0, 1, bottom, down),
                (0, 3, bottom, up),
                (0, 1, top, down),
                (3, 2, top, up),
                (1, 2, bottom, down),
            ]
        out, arrive = [], []
        for number, (sent, got, rows, peer) in enumerate(moves):
            mine = segment(piece, stage, sent, rows)
            theirs = segment(piece, stage, got, rows)
            out.append(send(mine, mine, w_sems, base + number, peer))
            arrive.append(send(theirs, theirs, w_sems, base + number, peer))
        return out, arrive

    w_plan = [[w_copies(piece, stage) for stage in range(3)] for piece in range(3)]

    def w_begin(stage):
        for number in range(3 if stage < 2 else 4):
            for piece in range(3):
                w_plan[piece][stage][0][number].start()

    def w_end(stage):
        for piece in range(3):
            for number in (0, 1, 2) if stage < 2 else (2, 3, 4, 5):
                w_plan[piece][stage][1][number].wait_recv()

    def w_forward(piece):
        out, arrive = w_plan[piece][2]
        arrive[0].wait_recv()
        out[4].start()
        arrive[1].wait_recv()
        out[5].start()

    kv_sems = (kv_send, kv_recv)

    def kv_block(dy, dx):
        return lax.rem(x_low + dx, 2) * 4 + lax.rem(y + dy, 4)

    def kv_copy(number, block, part, peer):
        ref = kv.at[block] if part is None else kv.at[block, part]
        return send(ref, ref, kv_sems, number, peer)

    kv_out = (
        kv_copy(0, kv_block(0, 0), None, y_up),
        kv_copy(1, kv_block(0, 0), None, y_down),
        kv_copy(2, kv_block(0, 0), None, partner),
        kv_copy(3, kv_block(3, 0), 0, y_up),
        kv_copy(4, kv_block(1, 0), 1, y_down),
        kv_copy(5, kv_block(0, 1), None, y_up),
        kv_copy(6, kv_block(0, 1), None, y_down),
        kv_copy(7, kv_block(2, 0), None, partner),
    )
    kv_in = (
        kv_copy(0, kv_block(3, 0), None, y_up),
        kv_copy(1, kv_block(1, 0), None, y_down),
        kv_copy(2, kv_block(0, 1), None, partner),
        kv_copy(3, kv_block(2, 0), 0, y_up),
        kv_copy(4, kv_block(2, 0), 1, y_down),
        kv_copy(5, kv_block(3, 1), None, y_up),
        kv_copy(6, kv_block(1, 1), None, y_down),
        kv_copy(7, kv_block(2, 1), None, partner),
    )

    loads[0].wait()
    w_begin(0)
    loads[1].wait()
    loads[2].wait()
    for number in (0, 1, 2):
        kv_out[number].start()
    expert_loads = []
    for number, (src, dst) in enumerate(((gate_hbm, gate_w), (up_hbm, up_w), (down_hbm, down_w))):
        expert_loads.append(pltpu.make_async_copy(src, dst, expert_sem.at[number]))
        expert_loads[-1].start()

    loads[3].wait()
    loads[4].wait()
    shares = gates[...] / jnp.sum(gates[...], axis=0, keepdims=True)
    ids_here = ids[...]
    expert_row = lax.broadcasted_iota(jnp.int32, (EXPERTS, TOK), 0)
    dense = jnp.zeros((EXPERTS, TOK), jnp.float32)
    for k in range(TOPK):
        dense = dense + jnp.where(ids_here[k : k + 1] == expert_row, shares[k : k + 1], 0.0)
    for group in range(4):
        share_tiles[group] = dense[group * 8 : (group + 1) * 8]
    shares_in[exp] = share_tiles[exp // 4]
    share_sems = (share_send, share_recv)
    share_out, share_arrive = [], []
    for step in range(1, 16):
        there = lax.rem(exp + step, 16)
        behind = lax.rem(exp + 16 - step, 16)
        peer = {"ctx": ctx, "exp": there}
        tile = share_tiles.at[there // 4]
        share_out.append(send(tile, shares_in.at[exp], share_sems, step, peer))
        share_arrive.append(send(tile, shares_in.at[behind], share_sems, step, peer))

    w_end(0)
    w_begin(1)
    for copy in share_out:
        copy.start()
    for number in (0, 1, 2):
        kv_in[number].wait_recv()
    for number in (3, 4, 5, 6):
        kv_out[number].start()
    w_end(1)
    w_begin(2)
    kv_in[3].wait_recv()
    kv_in[4].wait_recv()
    kv_out[7].start()
    for arriving in share_arrive:
        arriving.wait_recv()
    lane = lax.broadcasted_iota(jnp.int32, (TOK, TOK), 1)
    row = lax.broadcasted_iota(jnp.int32, (TOK, TOK), 0)
    up_to = (row <= lane).astype(jnp.float32).astype(jnp.bfloat16)
    slot_of_row = lax.rem(row, CAP).astype(jnp.float32)
    first_row = lax.rem(exp, 4) * 2

    def selection(block, carry):
        share_rows = jnp.concatenate(
            [
                jnp.broadcast_to(shares_in[block, pl.ds(first_row + j, 1)], (CAP, TOK))
                for j in range(2)
            ],
            axis=0,
        )
        chosen = share_rows > 0.0
        count = jnp.dot(
            chosen.astype(jnp.float32).astype(jnp.bfloat16),
            up_to,
            preferred_element_type=jnp.float32,
        )
        picked = chosen & (count - 1.0 == slot_of_row)
        pick[block] = picked.astype(jnp.float32).astype(jnp.bfloat16)
        scatter[block] = jnp.where(picked, share_rows, 0.0).T.astype(jnp.bfloat16)
        return carry

    lax.fori_loop(0, 16, selection, 0)

    for piece in range(3):
        w_forward(piece)
    for number in (5, 6, 7):
        kv_in[number].wait_recv()
    for copy in query_loads:
        copy.wait()

    att_sems = (att_send, att_recv)

    def att_copy(number):
        part = attended.at[core, :, pl.ds(pl.multiple_of(number * 512, 512), 512)]
        return send(part, part, att_sems, number, sibling)

    keys_total = 8 * TOK
    scale = HEAD_SIZE**-0.5 * 1.4426950408889634

    def heads(quad, carry):
        lanes = pl.ds(pl.multiple_of((quad // 2) * HEAD_SIZE, HEAD_SIZE), HEAD_SIZE)
        keys_here = jnp.concatenate([kv[block, 0, :, lanes] for block in range(8)], axis=0)
        values_here = jnp.concatenate([kv[block, 1, :, lanes] for block in range(8)], axis=0)
        values_wide = jnp.concatenate([values_here, jnp.ones_like(values_here)], axis=1)
        for part in range(4):
            scores = lax.dot_general(
                stacked[quad, part * TOK : (part + 1) * TOK],
                keys_here,
                (((1,), (1,)), ((), ())),
                preferred_element_type=jnp.float32,
            )
            query_at = lax.broadcasted_iota(jnp.int32, (TOK, keys_total), 0) + ctx * TOK
            key_at = lax.broadcasted_iota(jnp.int32, (TOK, keys_total), 1)
            scores = jnp.where(query_at >= key_at, scores, mask_fill_value)
            top = jnp.max(scores, axis=1, keepdims=True)
            weights = jnp.exp2((scores - top) * scale).astype(jnp.bfloat16)
            result = jnp.dot(weights, values_wide, preferred_element_type=jnp.float32)
            attended[
                core,
                :,
                pl.ds(pl.multiple_of(quad * 512 + part * HEAD_SIZE, HEAD_SIZE), HEAD_SIZE),
            ] = (result[:, :HEAD_SIZE] / result[:, HEAD_SIZE:]).astype(jnp.bfloat16)
        att_copy(quad).start()
        return carry

    lax.fori_loop(0, 8, heads, 0)

    for number in range(8):
        part = attended.at[other, :, pl.ds(number * 512, 512)]
        send(part, part, att_sems, number, sibling).wait_recv()
    w_end(2)

    def project(whose):
        def run(half, carry):
            target, at = (to_sibling, half) if whose is other else (from_sibling, 2 + half)
            target[at] = jnp.dot(
                attended[whose],
                weight[half].reshape(8 * 512, 512),
                preferred_element_type=jnp.float32,
            )
            return carry

        lax.fori_loop(0, 2, run, 0)

    project(other)
    swap = send(to_sibling, from_sibling.at[pl.ds(0, 2)], (proj_send, proj_recv), 0, sibling)
    swap.start()
    project(core)
    loads[5].wait()
    loads[6].wait()

    def place(first, which):
        for half in range(2):
            for depth in range(4):
                lanes = pl.ds(
                    pl.multiple_of(depth * 512 + half * 256 + which * 128, 128), 128
                )
                attn_resid_ref[:, lanes] = (
                    resid[:, lanes].astype(jnp.float32)
                    + from_sibling[first + half, :, depth * 128 : (depth + 1) * 128]
                ).astype(jnp.bfloat16)

    place(2, core)
    swap.wait_recv()
    place(0, other)
    wide = attn_resid_ref[...].astype(jnp.float32)
    scale_row = lax.rsqrt(jnp.mean(wide * wide, axis=1, keepdims=True) + norm_eps)
    blocks[exp] = (wide * scale_row * gain[...]).astype(jnp.bfloat16)

    def block_of(relation, which):
        dz, dx = RELATIONS[relation]
        return lax.rem(z + dz, 4) * 4 + lax.rem(x_high + dx, 2) * 2 + which

    ag = (ag_send, ag_recv)
    sib = (sib_send, sib_recv)
    low, high = pl.ds(0, CAP), pl.ds(CAP, CAP)

    def whole(relation):
        return blocks.at[block_of(relation, core)]

    def half_of(relation, rows):
        return blocks.at[block_of(relation, core), rows]

    quarters = [pl.ds(n * 32, 32) for n in range(4)]
    z_moves = (
        (0, low, 1, z_up),
        (0, high, 2, z_down),
        (0, None, 3, x_over),
        (0, high, 1, z_up),
        (0, low, 2, z_down),
        (1, quarters[0], 4, z_up),
        (2, quarters[2], 4, z_down),
        (1, quarters[1], 4, z_up),
        (2, quarters[3], 4, z_down),
        (3, None, 5, z_up),
        (3, None, 6, z_down),
        (4, quarters[0], 7, x_over),
        (4, quarters[2], 7, x_over),
        (4, quarters[1], 7, x_over),
        (4, quarters[3], 7, x_over),
    )
    ag_out, ag_in = [], []
    for number, (sent, rows, got, peer) in enumerate(z_moves):
        mine = whole(sent) if rows is None else half_of(sent, rows)
        theirs = whole(got) if rows is None else half_of(got, rows)
        ag_out.append(send(mine, mine, ag, number, peer))
        ag_in.append(send(theirs, theirs, ag, number, peer))
    sib_out = [send(whole(k), whole(k), sib, k, sibling) for k in range(8)]
    sib_in = []
    for k in range(8):
        arriving = blocks.at[block_of(k, other)]
        sib_in.append(send(arriving, arriving, sib, k, sibling))

    for number in range(5):
        ag_out[number].start()
    sib_out[0].start()
    for copy in expert_loads:
        copy.wait()
    for piece in range(3):
        for stage in range(3):
            for copy in w_plan[piece][stage][0]:
                copy.wait_send()

    def part_of(block):
        return weight.at[block // 8, lax.rem(block // 4, 2), lax.rem(block, 4)]

    def part_rows(block, rows):
        return weight.at[block // 8, lax.rem(block // 4, 2), lax.rem(block, 4), rows]

    part = (part_send, part_recv)
    rs = (rs_send, rs_recv)
    left, right = pl.ds(0, 256), pl.ds(256, 256)
    both = pl.ds(0, 512)

    def part_copy(chip):
        return send(part_of(chip * 2 + other), sib_parts.at[chip], part, chip, sibling)

    def add_into(block, rows, extra):
        target = part_rows(block, rows)
        target[...] = (target[...].astype(jnp.float32) + extra[...].astype(jnp.float32)).astype(
            jnp.bfloat16
        )

    def chip_sum(relation):
        chip = block_of(relation, 0) // 2
        part_copy(chip).wait_recv()
        add_into(chip * 2 + core, both, sib_parts.at[chip])

    def toward(relation, rows):
        return part_rows(block_of(relation, core), rows)

    fourths = [pl.ds(n * TOK, TOK) for n in range(4)]
    rs_out = []

    def rs_send_rows(relation, rows, into, peer):
        rs_out.append(send(toward(relation, rows), into, rs, len(rs_out), peer))

    def quarter_in(n):
        return half_in.at[n // 2, pl.ds(n % 2 * TOK, TOK)]

    z_way = (z_down, z_down, z_up, z_up)
    for n, rows in enumerate(fourths):
        rs_send_rows(4, rows, quarter_in(n), z_way[n])
    rs_send_rows(1, fourths[2], full_in.at[0, fourths[2]], z_down)
    rs_send_rows(2, fourths[1], full_in.at[1, fourths[1]], z_up)
    for n, rows in enumerate(fourths):
        rs_send_rows(1 + n // 2, rows, full_in.at[n // 2, rows], z_way[n])
    for n, rows in enumerate(fourths):
        rs_send_rows(7, rows, hop_in.at[rows], z_way[n])
    rs_send_rows(5, fourths[2], full_in.at[2, fourths[2]], z_down)
    rs_send_rows(6, fourths[1], full_in.at[3, fourths[1]], z_up)
    for n, rows in enumerate(fourths):
        rs_send_rows(5 + n // 2, rows, full_in.at[2 + n // 2, rows], z_way[n])
    for rows in fourths:
        rs_send_rows(3, rows, far_in.at[rows], x_over)
    rs_send_rows(5, fourths[3], x_in.at[0], x_over)
    rs_send_rows(6, fourths[0], x_in.at[1], x_over)
    rs_send_rows(1, fourths[3], full_in.at[0, fourths[3]], z_down)
    rs_send_rows(2, fourths[0], full_in.at[1, fourths[0]], z_up)

    def beside(n):
        rs_out[n].wait_recv()
        add_into(block_of(1 + n // 2, core), fourths[n], quarter_in(n))
        rs_out[6 + n].start()

    def beside_other(n):
        rs_out[10 + n].wait_recv()
        add_into(block_of(5 + n // 2, core), fourths[n], hop_in.at[fourths[n]])
        rs_out[16 + n].start()

    def across(n, which, numbers):
        for number in numbers:
            rs_out[number].wait_recv()
        target = toward(3, fourths[n])
        total = target[...].astype(jnp.float32)
        for k in which:
            total = total + full_in[k, fourths[n]].astype(jnp.float32)
        target[...] = total.astype(jnp.bfloat16)
        rs_out[20 + n].start()

    def joined(k):
        rs_out[24 + k].wait_recv()
        add_into(block_of(1 + k, core), fourths[3 - 3 * k], x_in.at[k])
        rs_out[26 + k].start()

    def step(number, carry):
        @pl.when(number == 0)
        def _():
            sib_in[0].wait_recv()

        @pl.when(number == 1)
        def _():
            ag_in[0].wait_recv()
            ag_out[5].start()
            ag_out[7].start()
            ag_in[1].wait_recv()
            ag_out[6].start()
            ag_out[8].start()
            ag_in[3].wait_recv()
            sib_out[1].start()
            ag_in[4].wait_recv()
            sib_out[2].start()
            ag_in[2].wait_recv()
            sib_out[3].start()
            sib_in[1].wait_recv()

        @pl.when(number == 2)
        def _():
            for k in (5, 6):
                ag_in[k].wait_recv()
                ag_out[k + 6].start()
            ag_out[9].start()
            ag_out[10].start()
            sib_in[2].wait_recv()

        @pl.when(number == 3)
        def _():
            for k in (7, 8):
                ag_in[k].wait_recv()
                ag_out[k + 6].start()
            sib_out[4].start()
            sib_in[3].wait_recv()

        @pl.when(number == 4)
        def _():
            sib_in[4].wait_recv()

        @pl.when(number == 5)
        def _():
            chip_sum(1)
            chip_sum(2)
            ag_in[9].wait_recv()
            sib_out[5].start()
            ag_in[10].wait_recv()
            sib_out[6].start()
            chip_sum(4)
            for n in (0, 2, 1, 3, 4, 5):
                rs_out[n].start()
            for k in (11, 12, 13, 14):
                ag_in[k].wait_recv()
            sib_out[7].start()
            sib_in[7].wait_recv()

        @pl.when(number == 6)
        def _():
            sib_in[5].wait_recv()

        @pl.when(number == 7)
        def _():
            sib_in[6].wait_recv()

        dz, dx = 0, 0
        for k, relation in enumerate(ORDER):
            dz = jnp.where(number == k, RELATIONS[relation][0], dz)
            dx = jnp.where(number == k, RELATIONS[relation][1], dx)
        chip = lax.rem(z + dz, 4) * 2 + lax.rem(x_high + dx, 2)
        for q in range(2):
            found = jnp.dot(
                pick[chip * 2 + q], blocks[chip * 2 + q], preferred_element_type=jnp.float32
            ).astype(jnp.bfloat16)
            for j in range(2):
                slots_in[j, q * CAP : (q + 1) * CAP] = found[j * CAP : (j + 1) * CAP]

        @pl.when(number == 6)
        def _():
            chip_sum(7)
            for n in (0, 2, 1, 3):
                rs_out[10 + n].start()
            beside(0)
            beside(2)

        @pl.when(number == 7)
        def _():
            chip_sum(5)
            rs_out[14].start()
            rs_out[24].start()
            beside(1)
            beside(3)

        def expert(j, carry):
            for n in range(3):
                cols = slice(n * 256, (n + 1) * 256)
                gate_part = jnp.dot(
                    slots_in[j], gate_w[j, :, cols], preferred_element_type=jnp.float32
                )
                up_part = jnp.dot(
                    slots_in[j], up_w[j, :, cols], preferred_element_type=jnp.float32
                )
                act[:, cols] = (gate_part / (1.0 + jnp.exp(-gate_part)) * up_part).astype(
                    jnp.bfloat16
                )
            for n in range(4):
                cols = slice(n * 512, (n + 1) * 512)
                result = jnp.dot(act[...], down_w[j, :, cols], preferred_element_type=jnp.float32)
                for q in range(2):
                    slots_out[q, pl.ds(pl.multiple_of(j * CAP, CAP), CAP), cols] = result[
                        q * CAP : (q + 1) * CAP
                    ].astype(jnp.bfloat16)
            return carry

        lax.fori_loop(0, 2, expert, 0)
        for which in (other, core):
            target = part_of(chip * 2 + which)
            for n in range(4):
                target[n * TOK : (n + 1) * TOK] = jnp.dot(
                    scatter[chip * 2 + which],
                    slots_out[which, :, n * 512 : (n + 1) * 512],
                    preferred_element_type=jnp.float32,
                ).astype(jnp.bfloat16)
            if which is other:
                part_copy(chip).start()
        return carry

    lax.fori_loop(0, 8, step, 0)

    chip_sum(6)
    rs_out[25].start()
    rs_out[15].start()
    for n in (0, 2, 1, 3):
        beside_other(n)
    chip_sum(3)
    chip_sum(0)
    joined(0)
    across(0, (2,), (16,))
    joined(1)
    across(2, (2, 3), (14, 18))
    across(1, (2, 3), (15, 17))
    across(3, (3,), (19,))

    arrivals = ((6, 27, 20), (7, 5, 21), (4, 8, 22), (26, 9, 23))
    for n in (0, 2, 1, 3):
        rows = slice(n * TOK, (n + 1) * TOK)
        cols = slice(n * 512, (n + 1) * 512)
        for number in arrivals[n]:
            rs_out[number].wait_recv()
        total = attn_resid_ref[:, cols].astype(jnp.float32)
        for extra in (part_of(exp), full_in.at[0], full_in.at[1], far_in):
            total = total + extra[rows].astype(jnp.float32)
        out_ref[:, cols] = total.astype(jnp.bfloat16)

    for copy in (*kv_out, *share_out, swap, *ag_out, *sib_out, *rs_out):
        copy.wait_send()
    for number in range(8):
        att_copy(number).wait_send()
        part_copy(number).wait_send()


def layer(*arrays):
    vmem = pl.BlockSpec(memory_space=pltpu.VMEM)
    hbm = pl.BlockSpec(memory_space=pl.ANY)
    dma = pltpu.SemaphoreType.DMA
    bf16, f32 = jnp.bfloat16, jnp.float32
    counts = (7, 32, 3, 8, 8, 36, 36, 16, 16, 8, 8, 1, 1, 15, 15, 8, 8, 8, 8, 28, 28)
    return pl.pallas_call(
        layer_kernel,
        out_shape=jax.ShapeDtypeStruct((2, TOK, D), bf16),
        in_specs=[hbm] * 11,
        out_specs=vmem,
        scratch_shapes=[
            pltpu.VMEM((2, 2, 4, 512, 512), bf16),
            pltpu.VMEM((8, 2, TOK, 512), bf16),
            pltpu.VMEM((8, 512, HEAD_SIZE), bf16),
            pltpu.VMEM((2, TOK, 4096), bf16),
            pltpu.VMEM((2, TOK, 512), f32),
            pltpu.VMEM((4, TOK, 512), f32),
            pltpu.VMEM((TOK, D), bf16),
            pltpu.VMEM((1, D), f32),
            pltpu.VMEM((TOPK, TOK), jnp.int32),
            pltpu.VMEM((TOPK, TOK), f32),
            pltpu.VMEM((4, 8, TOK), f32),
            pltpu.VMEM((16, 8, TOK), f32),
            pltpu.VMEM((2, D, FF), bf16),
            pltpu.VMEM((2, D, FF), bf16),
            pltpu.VMEM((2, FF, D), bf16),
            pltpu.VMEM((16, TOK, D), bf16),
            pltpu.VMEM((8, 512, 512), bf16),
            pltpu.VMEM((2, 256, 512), bf16),
            pltpu.VMEM((4, 512, 512), bf16),
            pltpu.VMEM((512, 512), bf16),
            pltpu.VMEM((512, 512), bf16),
            pltpu.VMEM((2, TOK, 512), bf16),
            pltpu.VMEM((2, TOK, D), bf16),
            pltpu.VMEM((2, TOK, D), bf16),
            pltpu.VMEM((TOK, FF), bf16),
            pltpu.VMEM((16, TOK, TOK), bf16),
            pltpu.VMEM((16, TOK, TOK), bf16),
            *(dma((count,)) for count in counts),
        ],
        compiler_params=pltpu.CompilerParams(
            collective_id=0, has_side_effects=True, vmem_limit_bytes=62 << 20
        ),
    )(*arrays)


def local(
    queries,
    keys,
    values,
    resid,
    out_weight,
    norm_gain,
    expert_gate,
    expert_up,
    expert_down,
    route_ids,
    route_gates,
):
    outs = layer(
        queries[0],
        keys[0],
        values[0],
        resid[0],
        out_weight,
        norm_gain[None],
        route_ids[0].T,
        route_gates[0].T,
        expert_gate,
        expert_up,
        expert_down,
    )
    return (outs[0][None], outs[1][None])


def solution(mesh):
    in_specs = (
        P("exp", "ctx", None),
        P("exp", "ctx", None),
        P("exp", "ctx", None),
        P("exp", "ctx", None),
        P("ctx", "exp"),
        P(),
        P("exp", None, None),
        P("exp", None, None),
        P("exp", None, None),
        P("exp", "ctx", None),
        P("exp", "ctx", None),
    )
    out_specs = (P("exp", "ctx", None), P("exp", "ctx", None))
    return jax.shard_map(local, mesh=mesh, in_specs=in_specs, out_specs=out_specs, check_vma=False)
```
